32 devices in a mesh: dp: 8 (over y, x, core), tensor: 4 (over z).
Axes of the slice: x: 2, y: 2, z: 4, core: 2. Of those that a mesh axis runs over, the one named last changes fastest.
Arguments:
- hidden: bfloat16 [1536, 16384], P('dp', 'tensor'), may hold values from -6 to 6
- cotangent: bfloat16 [1536, 16384], P('dp', 'tensor'), may hold values from -6 to 6
- blocks: bfloat16 [7, 64, 256, 256], P(None, 'tensor', 'dp'), may hold values from -0.125 to 0.125
- low_left: bfloat16 [16384, 128], P('tensor'), may hold values from -0.046875 to 0.046875
- low_right: bfloat16 [128, 16384], P(None, 'tensor'), may hold values from -0.5 to 0.5
Outputs:
- mixed_rows: bfloat16 [1536, 16384], P('dp', 'tensor')
- grad_hidden: bfloat16 [1536, 16384], P('dp', 'tensor')
- grad_blocks: float32 [7, 64, 256, 256], P(None, 'tensor', 'dp')
- grad_left: float32 [16384, 128], P('tensor')
- grad_right: float32 [128, 16384], P(None, 'tensor')
The draws below stay inside these ranges and needn't reach their ends.
All inputs are finite; a program needn't handle non-finite values.
Results may differ from the reference program's by a relative error of at most 0.0095.
Values may be sent and summed in bfloat16 or wider, within the bound.
No kernel may reach another device: no remote copies, remote signals or barrier semaphores. Data moves between devices by JAX's collectives and lax.ppermute only.
A program may use at most 256 MiB of HBM per device.

```python
import jax
import jax.numpy as jnp
from jax import lax

FF = 16384
BLK = 256
RANK = 128
LEVELS = 6
TOK_DEV = 192
NB = 64
TERMS = 7
TOKENS = 1536
N_DP = 8


def steps_of(rng, dims, pieces, low, largest):
    factor_of = 1.0
    for position, parts in pieces:
        draws = jax.random.uniform(jax.random.fold_in(jax.random.fold_in(rng, 6), position), (parts,), jnp.float32, low / len(pieces), largest / len(pieces))
        factor_of = factor_of * jnp.repeat(jnp.exp(draws), dims[position] // parts).reshape((-1,) + (1,) * (len(dims) - 1 - position))
    return factor_of


def bell_draw(rng, extent, spread, limit, cuts=(), kind=jnp.bfloat16):
    values = spread * jax.random.normal(rng, extent, jnp.float32)
    if cuts:
        values = values * steps_of(rng, extent, cuts, -0.22, 0.18)
    return jnp.clip(values, -limit, limit).astype(kind)


def setup_inputs(seed: int = 0) -> dict:
    key_of = jax.random.split(jax.random.key(seed), 6)
    return {
        "hidden": bell_draw(key_of[0], (TOKENS, FF), 1.0, 6.0, ((0, 8), (1, 4))),
        "cotangent": bell_draw(key_of[1], (TOKENS, FF), 1.0, 6.0, ((0, 8), (1, 4))),
        "blocks": bell_draw(key_of[2], (TERMS, NB, BLK, BLK), (TERMS * BLK) ** -0.5, 0.125, ((1, 4), (2, 8))),
        "low_left": bell_draw(key_of[3], (FF, RANK), FF ** -0.5, 0.046875, ((0, 4),)),
        "low_right": bell_draw(key_of[4], (RANK, FF), RANK ** -0.5, 0.5, ((1, 4),)),
    }


def flip_blocks(values, distance):
    array_shape = values.shape
    grouped = values.reshape(array_shape[:-2] + (array_shape[-2] // (2 * distance), 2, distance, array_shape[-1]))
    return grouped[..., ::-1, :, :].reshape(array_shape)

def reference(hidden, cotangent, blocks, low_left, low_right):
    grad_scale = jnp.float32(1.0) / jnp.sqrt(jnp.float32(TOKENS))
    block_weights = blocks.astype(jnp.float32)

    def one_shard(carried, shard_idx):
        grad_blocks, grad_left, grad_right = carried
        row_start = (shard_idx * TOK_DEV).astype(jnp.int32)
        rows_in = lax.dynamic_slice_in_dim(hidden, row_start, TOK_DEV, 0)
        rows_cot = lax.dynamic_slice_in_dim(cotangent, row_start, TOK_DEV, 0)
        inputs_f = rows_in.reshape(TOK_DEV, NB, BLK).astype(jnp.float32)
        cot_f = rows_cot.reshape(TOK_DEV, NB, BLK).astype(jnp.float32)
        sources = jnp.stack([inputs_f] + [flip_blocks(inputs_f, 2 ** level_idx) for level_idx in range(LEVELS)])
        mixed_blocks = jnp.einsum('ktnb,knbc->tnc', sources, block_weights, precision=lax.Precision.HIGHEST)
        factor_in = jnp.dot(rows_in, low_left, preferred_element_type=jnp.float32)
        factor_b = factor_in.astype(jnp.bfloat16)
        low_term = jnp.dot(factor_b, low_right, preferred_element_type=jnp.float32)
        mixed_rows = (mixed_blocks.reshape(TOK_DEV, FF) + low_term).astype(jnp.bfloat16)
        products = jnp.einsum('tnc,knbc->ktnb', cot_f, block_weights, precision=lax.Precision.HIGHEST)
        grad_in = products[0]
        for level_idx in range(LEVELS):
            grad_in = grad_in + flip_blocks(products[level_idx + 1], 2 ** level_idx)
        factor_back = jnp.dot(rows_cot, low_right.T, preferred_element_type=jnp.float32)
        back_b = factor_back.astype(jnp.bfloat16)
        grad_rows = (grad_in.reshape(TOK_DEV, FF) + jnp.dot(back_b, low_left.T, preferred_element_type=jnp.float32)).astype(jnp.bfloat16)
        part_blocks = jnp.einsum('ktnb,tnc->knbc', sources, cot_f, precision=lax.Precision.HIGHEST) * grad_scale
        part_blocks = lax.optimization_barrier(part_blocks.astype(jnp.bfloat16)).astype(jnp.float32)
        part_left = jnp.dot(rows_in.T, back_b, preferred_element_type=jnp.float32) * grad_scale
        part_right = jnp.dot(factor_b.T, rows_cot, preferred_element_type=jnp.float32) * grad_scale
        return ((grad_blocks + part_blocks, grad_left + part_left, grad_right + part_right), (mixed_rows, grad_rows))
    initial = (jnp.zeros(blocks.shape, jnp.float32), jnp.zeros(low_left.shape, jnp.float32), jnp.zeros(low_right.shape, jnp.float32))
    totals, outputs = lax.scan(one_shard, initial, jnp.arange(N_DP, dtype=jnp.int32))
    mixed_all = outputs[0].reshape(TOKENS, FF)
    grads_all = outputs[1].reshape(TOKENS, FF)
    return (mixed_all, grads_all, totals[0], totals[1], totals[2])
```

```python
import functools

import jax
import jax.numpy as jnp
from jax import lax
from jax.experimental import pallas as pl
from jax.experimental.pallas import tpu as pltpu
from jax.sharding import PartitionSpec as P

F32 = jnp.float32
BF16 = jnp.bfloat16
VMEM_LIMIT = 40 * 1024 * 1024


def swap(value, axis, mask):
    return lax.ppermute(value, axis, [(i, i ^ mask) for i in range(lax.axis_size(axis))])


def params():
    return pltpu.CompilerParams(
        dimension_semantics=("arbitrary",), vmem_limit_bytes=VMEM_LIMIT
    )


def aligned(index, size):
    return pl.ds(pl.multiple_of(index * size, size), size)


def grads_kernel(levels, shards, scale, pos_ref, cot_ref, *refs):
    n_src = 1 + max(src for src, _ in levels)
    sources, (keep_ref, send_ref, tmp_ref) = refs[:n_src], refs[n_src:]
    block = cot_ref.shape[1]
    rows = block // shards
    j = pl.program_id(0)
    pos = pos_ref[0]
    cot = cot_ref[...]
    for k, (src, distance) in enumerate(levels):
        values = sources[src][:, aligned(j ^ distance, block)]
        term = lax.dot_general(
            values, cot, (((0,), (0,)), ((), ())), preferred_element_type=F32
        )
        tmp_ref[k] = term * scale
        for m in range(shards):
            part = tmp_ref[k, aligned(pos ^ m, rows), :].astype(BF16)
            (send_ref if m & 1 else keep_ref)[m >> 1, k, 0] = part


def block_grads(pos, cot, sources, levels, n_blocks, shards, scale):
    tok, ff = cot.shape
    block = ff // n_blocks
    rows = block // shards
    part = jax.ShapeDtypeStruct((shards // 2, len(levels), n_blocks, rows, block), BF16)
    part_spec = pl.BlockSpec(
        (shards // 2, len(levels), 1, rows, block), lambda j, *_: (0, 0, j, 0, 0)
    )
    return pl.pallas_call(
        functools.partial(grads_kernel, levels, shards, scale),
        grid_spec=pltpu.PrefetchScalarGridSpec(
            num_scalar_prefetch=1,
            grid=(n_blocks,),
            in_specs=[pl.BlockSpec((tok, block), lambda j, *_: (0, j))]
            + [pl.BlockSpec((tok, ff), lambda j, *_: (0, 0)) for _ in sources],
            out_specs=[part_spec, part_spec],
            scratch_shapes=[pltpu.VMEM((len(levels), block, block), F32)],
        ),
        out_shape=[part, part],
        compiler_params=params(),
        cost_estimate=pl.CostEstimate(
            flops=2 * tok * ff * block * len(levels),
            bytes_accessed=2 * tok * ff * (1 + len(sources)) + 2 * len(levels) * ff * block,
            transcendentals=0,
        ),
    )(pos, cot, *sources)


def assemble(pos, pieces, refs, w_ref, k):
    for (m, columns, _), ref in zip(pieces, refs):
        w_ref[k, pos ^ m, :, columns] = ref[k, 0]
    shards, rows, block = w_ref.shape[1:]
    return w_ref[k].reshape(shards * rows, block)


def piece_specs(pieces):
    return [
        pl.BlockSpec((p.shape[0], 1) + p.shape[2:], lambda j, *_: (0, j, 0, 0))
        for _, _, p in pieces
    ]


def w_scratch(pieces, n_levels, shards):
    own = pieces[0][2]
    return pltpu.VMEM((n_levels, shards, own.shape[2], own.shape[3]), BF16)


NT = (((1,), (1,)), ((), ()))


def local_kernel(
    pieces, distances, pos_ref, hid_ref, cot_ref, fac_ref, back_ref, left_ref, right_ref, *refs
):
    w_refs, (mixed_ref, grad_ref, w_ref) = refs[: len(pieces)], refs[len(pieces) :]
    block = cot_ref.shape[1]
    j = pl.program_id(0)
    pos = pos_ref[0]

    @pl.when(j == 0)
    def _():
        grad_ref[...] = jnp.zeros_like(grad_ref)

    cot = cot_ref[...]
    mixed = jnp.dot(fac_ref[...], right_ref[...], preferred_element_type=F32)
    for k, distance in enumerate(distances):
        weight = assemble(pos, pieces, w_refs, w_ref, k)
        there = aligned(j ^ distance, block)
        mixed += jnp.dot(hid_ref[:, there], weight, preferred_element_type=F32)
        term = lax.dot_general(cot, weight, NT, preferred_element_type=F32)
        if distance == 0:
            term += lax.dot_general(back_ref[...], left_ref[...], NT, preferred_element_type=F32)
        grad_ref[:, there] += term
    mixed_ref[...] = mixed


def local_terms(pos, hidden, cot, factor, back, low_left, low_right, pieces, distances, n_blocks, shards):
    tok, ff = hidden.shape
    block = ff // n_blocks
    rank = factor.shape[1]
    column = pl.BlockSpec((tok, block), lambda j, *_: (0, j))
    whole = pl.BlockSpec((tok, ff), lambda j, *_: (0, 0))
    low = pl.BlockSpec((tok, rank), lambda j, *_: (0, 0))
    out = jax.ShapeDtypeStruct((tok, ff), F32)
    return pl.pallas_call(
        functools.partial(local_kernel, pieces, distances),
        grid_spec=pltpu.PrefetchScalarGridSpec(
            num_scalar_prefetch=1,
            grid=(n_blocks,),
            in_specs=[
                whole,
                column,
                low,
                low,
                pl.BlockSpec((block, rank), lambda j, *_: (j, 0)),
                pl.BlockSpec((rank, block), lambda j, *_: (0, j)),
            ]
            + piece_specs(pieces),
            out_specs=[column, whole],
            scratch_shapes=[w_scratch(pieces, len(distances), shards)],
        ),
        out_shape=[out, out],
        compiler_params=params(),
        cost_estimate=pl.CostEstimate(
            flops=4 * tok * ff * block * len(distances),
            bytes_accessed=12 * tok * ff + 2 * len(distances) * ff * block,
            transcendentals=0,
        ),
    )(pos, hidden, cot, factor, back, low_left, low_right, *[p for _, _, p in pieces])


def back_kernel(pieces, n_levels, pos_ref, cot_ref, *refs):
    w_refs, (out_refs, w_ref) = refs[: len(pieces)], (refs[len(pieces) : -1], refs[-1])
    for k in range(n_levels):
        weight = assemble(pos_ref[0], pieces, w_refs, w_ref, k)
        term = lax.dot_general(cot_ref[...], weight, NT, preferred_element_type=F32)
        out_refs[k][...] = term.astype(BF16)


def back_terms(pos, cot, pieces, n_levels, n_blocks, shards):
    tok, ff = cot.shape
    block = ff // n_blocks
    column = pl.BlockSpec((tok, block), lambda j, *_: (0, j))
    return pl.pallas_call(
        functools.partial(back_kernel, pieces, n_levels),
        grid_spec=pltpu.PrefetchScalarGridSpec(
            num_scalar_prefetch=1,
            grid=(n_blocks,),
            in_specs=[column] + piece_specs(pieces),
            out_specs=[column] * n_levels,
            scratch_shapes=[w_scratch(pieces, n_levels, shards)],
        ),
        out_shape=[jax.ShapeDtypeStruct((tok, ff), BF16)] * n_levels,
        compiler_params=params(),
        cost_estimate=pl.CostEstimate(
            flops=2 * tok * ff * block * n_levels,
            bytes_accessed=2 * tok * ff * (1 + n_levels) + 2 * n_levels * ff * block,
            transcendentals=0,
        ),
    )(pos, cot, *[p for _, _, p in pieces])


def cross_kernel(pieces, n_levels, pos_ref, mixed_ref, *refs):
    sources = refs[:n_levels]
    w_refs, (out_ref, w_ref) = refs[n_levels:-2], refs[-2:]
    mixed = mixed_ref[...]
    for k in range(n_levels):
        weight = assemble(pos_ref[0], pieces, w_refs, w_ref, k)
        mixed += jnp.dot(sources[k][...], weight, preferred_element_type=F32)
    out_ref[...] = mixed.astype(BF16)


def cross_terms(pos, mixed, sources, pieces, n_blocks, shards):
    tok, ff = mixed.shape
    block = ff // n_blocks
    n_levels = len(sources)
    column = pl.BlockSpec((tok, block), lambda j, *_: (0, j))
    return pl.pallas_call(
        functools.partial(cross_kernel, pieces, n_levels),
        grid_spec=pltpu.PrefetchScalarGridSpec(
            num_scalar_prefetch=1,
            grid=(n_blocks,),
            in_specs=[column] * (1 + n_levels) + piece_specs(pieces),
            out_specs=column,
            scratch_shapes=[w_scratch(pieces, n_levels, shards)],
        ),
        out_shape=jax.ShapeDtypeStruct((tok, ff), BF16),
        compiler_params=params(),
        cost_estimate=pl.CostEstimate(
            flops=2 * tok * ff * block * n_levels,
            bytes_accessed=2 * tok * ff * (3 + n_levels) + 2 * n_levels * ff * block,
            transcendentals=0,
        ),
    )(pos, mixed, *sources, *[p for _, _, p in pieces])


def highest(mask):
    return 1 << mask.bit_length() - 1


def gather_pieces(own, shards):
    half = own.shape[-1] // 2
    low, high, full = slice(0, half), slice(half, None), slice(None)
    far = {0: [(full, own)]}
    for mask in range(2, shards, 2):
        last_a, last_b = highest(mask), mask & -mask
        if last_a == last_b:
            far[mask] = [(full, swap(own, "dp", mask))]
            continue
        far[mask] = []
        for last, columns in ((last_a, low), (last_b, high)):
            for held, value in far[mask ^ last]:
                if held == full:
                    value = value[..., columns]
                elif held != columns:
                    continue
                far[mask].append((columns, swap(value, "dp", last)))
    pieces = [(mask, columns, value) for mask in far for columns, value in far[mask]]
    return pieces + [(mask | 1, columns, swap(value, "dp", 1)) for mask, columns, value in pieces]


def scatter_sum(keep, send, shards):
    arrived = swap(send, "dp", 1)
    half = keep.shape[-1] // 2
    bits = [bit for bit in range(shards.bit_length() - 2)]
    totals = []
    for columns, order in ((slice(0, half), bits), (slice(half, None), bits[::-1])):
        terms = {
            q: [keep[q][..., columns], arrived[q][..., columns]] for q in range(shards // 2)
        }
        for bit in order:
            got = {}
            for q in sorted(terms):
                if q >> bit & 1:
                    total = sum(t.astype(F32) for t in terms[q]).astype(BF16)
                    got[q ^ 1 << bit] = swap(total, "dp", 2 << bit)
            terms = {q: terms[q] + [got[q]] for q in terms if not q >> bit & 1}
        totals.append(sum(t.astype(F32) for t in terms[0]))
    return jnp.concatenate(totals, axis=-1)


def per_device(hidden, cotangent, blocks, low_left, low_right):
    tok, ff = hidden.shape
    n_blocks = blocks.shape[1]
    shards = lax.axis_size("dp")
    local_bits = n_blocks.bit_length() - 1
    cross_bits = lax.axis_size("tensor").bit_length() - 1
    n_local = 1 + local_bits
    scale = 1.0 / (tok * shards) ** 0.5
    pos = lax.axis_index("dp").astype(jnp.int32).reshape(1)

    factors = jnp.concatenate(
        [
            jnp.dot(hidden, low_left, preferred_element_type=F32),
            lax.dot_general(cotangent, low_right, NT, preferred_element_type=F32),
        ],
        axis=1,
    )
    for bit in range(cross_bits):
        factors = factors + swap(factors, "tensor", 1 << bit)
    factors = factors.astype(BF16)
    rank = low_left.shape[1]
    factor, back = factors[:, :rank], factors[:, rank:]

    remote = [swap(hidden, "tensor", 1 << bit) for bit in range(cross_bits)]
    cross_pieces = gather_pieces(blocks[n_local:], shards)
    local_pieces = gather_pieces(blocks[:n_local], shards)

    distances = [0] + [1 << level for level in range(local_bits)]
    keep, send = block_grads(
        pos, cotangent, [hidden], [(0, d) for d in distances], n_blocks, shards, scale
    )
    grads_local = scatter_sum(keep, send, shards)

    sent = back_terms(pos, cotangent, cross_pieces, cross_bits, n_blocks, shards)
    returned = [swap(term, "tensor", 1 << bit) for bit, term in enumerate(sent)]

    mixed, grad_in = local_terms(
        pos, hidden, cotangent, factor, back, low_left, low_right,
        local_pieces, distances, n_blocks, shards,
    )
    mixed_rows = cross_terms(pos, mixed, remote, cross_pieces, n_blocks, shards)

    keep, send = block_grads(
        pos, cotangent, remote, [(bit, 0) for bit in range(cross_bits)], n_blocks, shards, scale
    )
    grads_cross = scatter_sum(keep, send, shards)
    grad_blocks = jnp.concatenate([grads_local, grads_cross], axis=0)

    part_left = jnp.einsum("tf,tr->fr", hidden, back, preferred_element_type=F32) * scale
    part_right = jnp.einsum("tr,tf->rf", factor, cotangent, preferred_element_type=F32) * scale
    grad_left, grad_right = lax.psum((part_left, part_right), "dp")

    grad_hidden = (grad_in + sum(term.astype(F32) for term in returned)).astype(BF16)
    return (mixed_rows, grad_hidden, grad_blocks, grad_left, grad_right)


def solution(mesh):
    placed = (
        P("dp", "tensor"),
        P("dp", "tensor"),
        P(None, "tensor", "dp", None),
        P("tensor", None),
        P(None, "tensor"),
    )
    return jax.shard_map(
        per_device, mesh=mesh, in_specs=placed, out_specs=placed, check_vma=False
    )
```

```python
import functools

import jax
import jax.numpy as jnp
from jax import lax
from jax.experimental import pallas as pl
from jax.experimental.pallas import tpu as pltpu
from jax.sharding import PartitionSpec as P

F32 = jnp.float32
BF16 = jnp.bfloat16
COST = pl.CostEstimate(flops=1, bytes_accessed=1, transcendentals=0)
VMEM_LIMIT = 28 * 1024 * 1024


def swap(value, axis, mask):
    return lax.ppermute(value, axis, [(i, i ^ mask) for i in range(lax.axis_size(axis))])


def params():
    return pltpu.CompilerParams(
        dimension_semantics=("arbitrary",), vmem_limit_bytes=VMEM_LIMIT
    )


def aligned(index, size):
    return pl.ds(pl.multiple_of(index * size, size), size)


TN = (((0,), (0,)), ((), ()))
NT = (((1,), (1,)), ((), ()))


def after(value, *others):
    return lax.optimization_barrier((value, *others))[0]


def join(j, parts, refs, joined):
    @pl.when(j == 0)
    def _():
        places = iter(refs)
        start = 0
        for width, _ in parts:
            for to in joined:
                to[:, start : start + width] = next(places)[:, :width]
            start += width

    return joined


def grads_kernel(levels, parts, shards, scale, pos_ref, cot_ref, *refs):
    joined = len(parts[0][1])
    sources = join(pl.program_id(0), parts, refs[: len(refs) - 3 - joined], refs[len(refs) - joined :])
    keep_ref, send_ref, tmp_ref = refs[len(refs) - 3 - joined : len(refs) - joined]
    block = cot_ref.shape[1]
    rows = block // shards
    j = pl.program_id(0)
    pos = pos_ref[0]
    cot = cot_ref[...]
    for k in range(levels):
        values = sources[k][:, aligned(j, block)]
        tmp_ref[k] = lax.dot_general(values, cot, TN, preferred_element_type=F32) * scale
        for m in range(shards):
            part = tmp_ref[k, aligned(pos ^ m, rows), :].astype(BF16)
            (send_ref if m & 1 else keep_ref)[m >> 1, k, 0] = part


def block_grads(pos, cot, parts, n_blocks, shards, scale):
    tok, ff = cot.shape
    block = ff // n_blocks
    rows = block // shards
    n_levels = len(parts[0][1])
    sources = [value for _, part in parts for value in part]
    part = jax.ShapeDtypeStruct((shards // 2, n_levels, n_blocks, rows, block), BF16)
    part_spec = pl.BlockSpec(
        (shards // 2, n_levels, 1, rows, block), lambda j, *_: (0, 0, j, 0, 0)
    )
    return pl.pallas_call(
        functools.partial(grads_kernel, n_levels, parts, shards, scale),
        grid_spec=pltpu.PrefetchScalarGridSpec(
            num_scalar_prefetch=1,
            grid=(n_blocks,),
            in_specs=[pl.BlockSpec((tok, block), lambda j, *_: (0, j))]
            + [pl.BlockSpec(s.shape, lambda j, *_: (0, 0)) for s in sources],
            out_specs=[part_spec, part_spec],
            scratch_shapes=[pltpu.VMEM((n_levels, block, block), F32)]
            + [pltpu.VMEM((tok, ff), BF16)] * n_levels,
        ),
        out_shape=[part, part],
        compiler_params=params(),
        cost_estimate=COST,
    )(pos, cot, *sources)


def pair_kernel(distances, shards, scale, pos_ref, *refs):
    ins, (keep_ref, tmp_ref) = refs[:-2], refs[-2:]
    pair = ins[: len(ins) // 2], ins[len(ins) // 2 :]
    block = ins[1].shape[1]
    rows = block // shards
    j = pl.program_id(0)
    pos = pos_ref[0]

    def product(left, right):
        return lax.dot_general(left, right, TN, preferred_element_type=F32)

    for k, distance in enumerate((*distances, None)):
        if distance is None:
            rank = ins[2].shape[1] // 2
            tmp_ref[k, :, :rank] = scale * sum(
                product(hid[:, aligned(j, block)], fac[:, rank:]) for hid, _, fac in pair
            )
            tmp_ref[k, :, rank:] = scale * sum(
                product(cot[...], fac[:, :rank]) for _, cot, fac in pair
            )
        else:
            there = aligned(j ^ distance, block)
            tmp_ref[k] = scale * sum(product(hid[:, there], cot[...]) for hid, cot, _ in pair)
        for m in range(0, shards, 2):
            keep_ref[m >> 1, k, 0] = tmp_ref[k, aligned(pos ^ m, rows), :].astype(BF16)


def pair_grads(pos, mine, other, distances, n_blocks, shards, scale):
    tok, ff = mine[0].shape
    block = ff // n_blocks
    shape = (shards // 2, len(distances) + 1, n_blocks, block // shards, block)
    specs = [
        pl.BlockSpec((tok, ff), lambda j, *_: (0, 0)),
        pl.BlockSpec((tok, block), lambda j, *_: (0, j)),
        pl.BlockSpec(mine[2].shape, lambda j, *_: (0, 0)),
    ]
    return pl.pallas_call(
        functools.partial(pair_kernel, distances, shards, scale),
        grid_spec=pltpu.PrefetchScalarGridSpec(
            num_scalar_prefetch=1,
            grid=(n_blocks,),
            in_specs=specs
            + [
                pl.BlockSpec((None, tok, ff), lambda j, *_: (0, 0, 0)),
                pl.BlockSpec((None, tok, block), lambda j, *_: (1, 0, j)),
                specs[2],
            ],
            out_specs=pl.BlockSpec(shape[:2] + (1,) + shape[3:], lambda j, *_: (0, 0, j, 0, 0)),
            scratch_shapes=[pltpu.VMEM((shape[1], block, block), F32)],
        ),
        out_shape=jax.ShapeDtypeStruct(shape, BF16),
        compiler_params=params(),
        cost_estimate=COST,
    )(pos, *mine, *other)


def assemble(pos, pieces, refs, w_ref, k):
    for (masks, _), ref in zip(pieces, refs):
        for i, m in enumerate(masks):
            w_ref[k, pos ^ m] = ref[i, k, 0]
    shards, rows, block = w_ref.shape[1:]
    return w_ref[k].reshape(shards * rows, block)


def piece_specs(pieces, first, n_levels, start=0):
    return [
        pl.BlockSpec(
            tuple(map(pl.Element, (p.shape[0], n_levels, 1, p.shape[3], p.shape[4]))),
            lambda j, *_: (0, first, j + start, 0, 0),
        )
        for _, p in pieces
    ]


def w_scratch(pieces, n_levels, shards):
    return pltpu.VMEM((n_levels, shards) + pieces[0][1].shape[3:], BF16)


def rows_kernel(
    pieces, distances, parts, pos_ref, hid_ref, cot_ref, fac_ref, back_ref, left_ref, right_ref,
    *refs
):
    n_cross = len(parts[0][1])
    n_src = n_cross * len(parts)
    w_refs = refs[n_src : n_src + len(pieces)]
    mixed_ref, grad_ref, w_ref = refs[n_src + len(pieces) :][:3]
    block = cot_ref.shape[1]
    j = pl.program_id(0)
    pos = pos_ref[0]
    sources = join(j, parts, refs[:n_src], refs[-n_cross:])

    @pl.when(j == 0)
    def _():
        grad_ref[...] = jnp.zeros_like(grad_ref)

    cot = cot_ref[...]
    mixed = jnp.dot(fac_ref[...], right_ref[...], preferred_element_type=F32)
    for k, distance in enumerate(distances):
        weight = assemble(pos, pieces, w_refs, w_ref, k)
        there = aligned(j ^ distance, block)
        mixed += jnp.dot(hid_ref[:, there], weight, preferred_element_type=F32)
        term = lax.dot_general(cot, weight, NT, preferred_element_type=F32)
        if distance == 0:
            term += lax.dot_general(back_ref[...], left_ref[...], NT, preferred_element_type=F32)
        grad_ref[:, there] += term
    for k, source in enumerate(sources, len(distances)):
        weight = assemble(pos, pieces, w_refs, w_ref, k)
        mixed += jnp.dot(source[:, aligned(j, block)], weight, preferred_element_type=F32)
    mixed_ref[...] = mixed.astype(BF16)


def rows_terms(pos, hidden, cot, factor, back, low_left, low_right, parts, pieces, distances, n_blocks, shards):
    tok, ff = hidden.shape
    block = ff // n_blocks
    rank = factor.shape[1]
    n_cross = len(parts[0][1])
    n_levels = len(distances) + n_cross
    column = pl.BlockSpec((tok, block), lambda j, *_: (0, j))
    whole = pl.BlockSpec((tok, ff), lambda j, *_: (0, 0))
    low = pl.BlockSpec((tok, rank), lambda j, *_: (0, 0))
    sources = [value for _, part in parts for value in part]
    return pl.pallas_call(
        functools.partial(rows_kernel, pieces, distances, parts),
        grid_spec=pltpu.PrefetchScalarGridSpec(
            num_scalar_prefetch=1,
            grid=(n_blocks,),
            in_specs=[
                whole,
                column,
                low,
                low,
                pl.BlockSpec((block, rank), lambda j, *_: (j, 0)),
                pl.BlockSpec((rank, block), lambda j, *_: (0, j)),
            ]
            + [pl.BlockSpec(s.shape, lambda j, *_: (0, 0)) for s in sources]
            + piece_specs(pieces, 0, n_levels),
            out_specs=[column, whole],
            scratch_shapes=[w_scratch(pieces, n_levels, shards)]
            + [pltpu.VMEM((tok, ff), BF16)] * n_cross,
        ),
        out_shape=[jax.ShapeDtypeStruct((tok, ff), BF16), jax.ShapeDtypeStruct((tok, ff), F32)],
        compiler_params=params(),
        cost_estimate=COST,
    )(pos, hidden, cot, factor, back, low_left, low_right, *sources, *[p for _, p in pieces])


def back_kernel(pieces, n_levels, pos_ref, cot_ref, *refs):
    w_refs, (out_refs, w_ref) = refs[: len(pieces)], (refs[len(pieces) : -1], refs[-1])
    for k in range(n_levels):
        weight = assemble(pos_ref[0], pieces, w_refs, w_ref, k)
        term = lax.dot_general(cot_ref[...], weight, NT, preferred_element_type=F32)
        out_refs[k][...] = term.astype(BF16)


def back_terms(pos, cot, pieces, first, n_levels, shards, start, count):
    tok = cot.shape[0]
    block = pieces[0][1].shape[-1]
    column = pl.BlockSpec((tok, block), lambda j, *_: (0, j))
    return pl.pallas_call(
        functools.partial(back_kernel, pieces, n_levels),
        grid_spec=pltpu.PrefetchScalarGridSpec(
            num_scalar_prefetch=1,
            grid=(count,),
            in_specs=[pl.BlockSpec((tok, block), lambda j, *_: (0, j + start))]
            + piece_specs(pieces, first, n_levels, start),
            out_specs=[column] * n_levels,
            scratch_shapes=[w_scratch(pieces, n_levels, shards)],
        ),
        out_shape=[jax.ShapeDtypeStruct((tok, count * block), BF16)] * n_levels,
        compiler_params=params(),
        cost_estimate=COST,
    )(pos, cot, *[p for _, p in pieces])


def highest(mask):
    return 1 << mask.bit_length() - 1


def gather_pieces(own, shards, tie):
    half = own.shape[-1] // 2
    low, high, full = slice(0, half), slice(half, None), slice(None)
    far = {0: [(full, own)]}
    for mask in range(2, shards, 2):
        last_a, last_b = highest(mask), mask & -mask
        if last_a == last_b:
            far[mask] = [(full, swap(own, "dp", mask))]
            continue
        far[mask] = []
        for last, columns in ((last_a, low), (last_b, high)):
            for held, value in far[mask ^ last]:
                if held == full:
                    value = value[..., columns]
                elif held != columns:
                    continue
                far[mask].append((columns, swap(after(value, *tie), "dp", last)))
    near = [mask for mask in far if len(far[mask]) == 1]
    rest = [mask for mask in far if mask not in near]
    pieces = [(near, jnp.stack([far[mask][0][1] for mask in near]))]
    if rest:
        joined = [jnp.concatenate([value for _, value in far[mask]], axis=-1) for mask in rest]
        pieces.append((rest, jnp.stack(joined)))
    return pieces, [value for mask in far for _, value in far[mask]]


def with_pair(pieces, tie):
    return pieces + [
        ([mask | 1 for mask in masks], swap(after(value, *tie), "dp", 1))
        for masks, value in pieces
    ]


def scatter_sum(parts, shards, *ties):
    half = parts[0].shape[-1] // 2
    bits = list(range(shards.bit_length() - 2))
    totals, received = [], []
    for columns, order in ((slice(0, half), bits), (slice(half, None), bits[::-1])):
        terms = {
            q: [part[q][..., columns] for part in parts] for q in range(shards // 2)
        }
        for step, bit in enumerate(order):
            going = [q for q in sorted(terms) if q >> bit & 1]
            total = jnp.stack([sum(t.astype(F32) for t in terms[q]).astype(BF16) for q in going])
            if step < len(ties):
                total = after(total, *ties[step])
            got = swap(total, "dp", 2 << bit)
            terms = {q: terms[q] for q in terms if not q >> bit & 1}
            for place, q in enumerate(going):
                terms[q ^ 1 << bit] = terms[q ^ 1 << bit] + [got[place]]
        received.append(terms[0][-1])
        totals.append(sum(t.astype(F32) for t in terms[0]))
    return totals, received


def gather_rows(value, shards):
    pos = lax.axis_index("dp")
    for bit in range(shards.bit_length() - 1)[::-1]:
        other = swap(value, "dp", 1 << bit)
        first = pos >> bit & 1 == 0
        pair = jnp.where(first, value, other), jnp.where(first, other, value)
        value = jnp.stack(pair, axis=shards.bit_length() - 1 - bit)
    return value


def per_device(hidden, cotangent, blocks, low_left, low_right):
    tok, ff = hidden.shape
    n_blocks, block = blocks.shape[1], blocks.shape[3]
    shards = lax.axis_size("dp")
    local_bits = n_blocks.bit_length() - 1
    cross_bits = lax.axis_size("tensor").bit_length() - 1
    n_local = 1 + local_bits
    scale = 1.0 / (tok * shards) ** 0.5
    pos = lax.axis_index("dp").astype(jnp.int32).reshape(1)

    factors = jnp.concatenate(
        [
            jnp.dot(hidden, low_left, preferred_element_type=F32),
            lax.dot_general(cotangent, low_right, NT, preferred_element_type=F32),
        ],
        axis=1,
    ).astype(BF16)
    rank = low_left.shape[1]

    def add(value, other):
        return (value.astype(F32) + other.astype(F32)).astype(BF16)

    cuts = [0, max(1, n_blocks // 4) * block, max(2, n_blocks // 2) * block, ff]
    both = swap(jnp.stack([hidden, cotangent]), "dp", 1)
    remote, ready = [], []
    for number, (start, stop) in enumerate(zip(cuts, cuts[1:])):
        part = after(hidden[:, start:stop], *ready, *([both] if ready else []))
        ready = [
            swap(
                jnp.concatenate([part, factors], axis=1) if bit == number < 2 else part,
                "tensor",
                1 << bit,
            )
            for bit in range(cross_bits)
        ]
        remote.append((stop - start, ready))
        if number < 2:
            factors = add(factors, ready[number][:, stop - start :])
        if number == 1:
            for bit in range(2, cross_bits):
                factors = add(factors, swap(factors, "tensor", 1 << bit))
    factor, back = factors[:, :rank], factors[:, rank:]

    pieces, gathered = gather_pieces(blocks, shards, remote[0][1] + remote[1][1])
    direct = gathered[1:3]
    distances = [0] + [1 << level for level in range(local_bits)]
    their_factors = swap(after(factors, *direct, *remote[1][1]), "dp", 1)
    kept = pair_grads(
        pos, (hidden, cotangent, factors), (both, both, their_factors), distances, n_blocks,
        shards, scale,
    )

    pieces = with_pair(pieces, [their_factors])
    cuts = [0, max(1, n_blocks * 7 // 16), max(2, n_blocks * 3 // 4), n_blocks]
    sent, returned, ready = [], [], remote[-1][1]
    for number, (start, stop) in enumerate(zip(cuts, cuts[1:])):
        terms = back_terms(
            pos, after(cotangent, *(returned[0] if number > 1 else ())), pieces, n_local,
            cross_bits, shards, start, stop - start,
        )
        ready = [swap(after(t, *ready), "tensor", 1 << bit) for bit, t in enumerate(terms)]
        sent.append(list(terms))
        returned.append(ready)
    keep, send = block_grads(pos, after(cotangent, *sent[0]), remote, n_blocks, shards, scale)
    crossed = swap(send, "dp", 1)
    grads_local, received = scatter_sum(
        [kept], shards, gathered + remote[2][1], returned[0] + sent[1] + [keep]
    )
    mixed_rows, grad_in = rows_terms(
        pos, hidden, after(cotangent, crossed), factor, back, low_left, low_right, remote,
        pieces, distances, n_blocks, shards,
    )

    low = jnp.concatenate([part[n_local] for part in grads_local], axis=-1).astype(BF16)
    low = gather_rows(low, shards).reshape(ff, 2 * rank).astype(F32)
    grad_left, grad_right = low[:, :rank], low[:, rank:].T

    grads_cross, _ = scatter_sum(
        [keep, crossed], shards, received + returned[1] + sent[2] + [mixed_rows]
    )
    grad_blocks = jnp.concatenate(
        [
            jnp.concatenate([a[:n_local], b], axis=0)
            for a, b in zip(grads_local, grads_cross)
        ],
        axis=-1,
    )

    returned = [jnp.concatenate(pair, axis=1) for pair in zip(*returned)]
    grad_hidden = (grad_in + sum(term.astype(F32) for term in returned)).astype(BF16)
    return (mixed_rows, grad_hidden, grad_blocks, grad_left, grad_right)


def solution(mesh):
    placed = (
        P("dp", "tensor"),
        P("dp", "tensor"),
        P(None, "tensor", "dp", None),
        P("tensor", None),
        P(None, "tensor"),
    )
    return jax.shard_map(
        per_device, mesh=mesh, in_specs=placed, out_specs=placed, check_vma=False
    )
```

```python
import functools

import jax
import jax.numpy as jnp
from jax import lax
from jax.experimental import pallas as pl
from jax.experimental.pallas import tpu as pltpu
from jax.sharding import PartitionSpec as P

F32 = jnp.float32
BF16 = jnp.bfloat16
COST = pl.CostEstimate(flops=1, bytes_accessed=1, transcendentals=0)
VMEM_LIMIT = 28 * 1024 * 1024


def swap(value, axis, mask):
    return lax.ppermute(value, axis, [(i, i ^ mask) for i in range(lax.axis_size(axis))])


def params():
    return pltpu.CompilerParams(
        dimension_semantics=("arbitrary",), vmem_limit_bytes=VMEM_LIMIT
    )


def aligned(index, size):
    return pl.ds(pl.multiple_of(index * size, size), size)


TN = (((0,), (0,)), ((), ()))
NT = (((1,), (1,)), ((), ()))


def after(value, *others):
    return lax.optimization_barrier((value, *others))[0]


def join(j, parts, refs, joined):
    @pl.when(j == 0)
    def _():
        places = iter(refs)
        start = 0
        for width, _ in parts:
            for to in joined:
                to[:, start : start + width] = next(places)[:, :width]
            start += width

    return joined


def grads_kernel(n_parts, n_levels, shards, scale, pos_ref, *refs):
    cots, sources = refs[:n_parts], refs[n_parts:-3]
    keep_ref, send_ref, tmp_ref = refs[-3:]
    rows = cots[0].shape[1] // shards
    pos = pos_ref[0]
    for p, cot_ref in enumerate(cots):
        for k in range(n_levels):
            values = sources[p * n_levels + k][...]
            term = lax.dot_general(values, cot_ref[...], TN, preferred_element_type=F32)
            tmp_ref[p, k] = term * scale
            for m in range(shards):
                part = tmp_ref[p, k, aligned(pos ^ m, rows), :].astype(BF16)
                (send_ref if m & 1 else keep_ref)[m >> 1, k, p, 0] = part


def block_grads(pos, cot, parts, n_blocks, shards, scale):
    tok, ff = cot.shape
    block = ff // n_blocks
    rows = block // shards
    n_parts, n_levels = len(parts), len(parts[0][1])
    steps = n_blocks // n_parts
    part = jax.ShapeDtypeStruct((shards // 2, n_levels, n_parts, steps, rows, block), BF16)
    part_spec = pl.BlockSpec(
        (shards // 2, n_levels, n_parts, 1, rows, block), lambda j, *_: (0, 0, 0, j, 0, 0)
    )
    outs = pl.pallas_call(
        functools.partial(grads_kernel, n_parts, n_levels, shards, scale),
        grid_spec=pltpu.PrefetchScalarGridSpec(
            num_scalar_prefetch=1,
            grid=(steps,),
            in_specs=[
                pl.BlockSpec((tok, block), lambda j, *_, p=p: (0, p * steps + j))
                for p in range(n_parts)
            ]
            + [pl.BlockSpec((tok, block), lambda j, *_: (0, j))] * (n_parts * n_levels),
            out_specs=[part_spec, part_spec],
            scratch_shapes=[pltpu.VMEM((n_parts, n_levels, block, block), F32)],
        ),
        out_shape=[part, part],
        compiler_params=params(),
        cost_estimate=COST,
    )(pos, *[cot] * n_parts, *[value for _, part in parts for value in part])
    return [o.reshape(o.shape[:2] + (n_blocks,) + o.shape[4:]) for o in outs]


def pair_kernel(distances, shards, scale, pos_ref, *refs):
    ins, (keep_ref, tmp_ref) = refs[:-2], refs[-2:]
    pair = ins[: len(ins) // 2], ins[len(ins) // 2 :]
    block = ins[1].shape[1]
    rows = block // shards
    j = pl.program_id(0)
    pos = pos_ref[0]

    def product(left, right):
        return lax.dot_general(left, right, TN, preferred_element_type=F32)

    for k, distance in enumerate((*distances, None)):
        if distance is None:
            rank = ins[2].shape[1] // 2
            tmp_ref[k, :, :rank] = scale * sum(
                product(hid[:, aligned(j, block)], fac[:, rank:]) for hid, _, fac in pair
            )
            tmp_ref[k, :, rank:] = scale * sum(
                product(cot[...], fac[:, :rank]) for _, cot, fac in pair
            )
        else:
            there = aligned(j ^ distance, block)
            tmp_ref[k] = scale * sum(product(hid[:, there], cot[...]) for hid, cot, _ in pair)
        for m in range(0, shards, 2):
            keep_ref[m >> 1, k, 0] = tmp_ref[k, aligned(pos ^ m, rows), :].astype(BF16)


def pair_grads(pos, mine, other, distances, n_blocks, shards, scale):
    tok, ff = mine[0].shape
    block = ff // n_blocks
    shape = (shards // 2, len(distances) + 1, n_blocks, block // shards, block)
    specs = [
        pl.BlockSpec((tok, ff), lambda j, *_: (0, 0)),
        pl.BlockSpec((tok, block), lambda j, *_: (0, j)),
        pl.BlockSpec(mine[2].shape, lambda j, *_: (0, 0)),
    ]
    return pl.pallas_call(
        functools.partial(pair_kernel, distances, shards, scale),
        grid_spec=pltpu.PrefetchScalarGridSpec(
            num_scalar_prefetch=1,
            grid=(n_blocks,),
            in_specs=specs
            + [
                pl.BlockSpec((None, tok, ff), lambda j, *_: (0, 0, 0)),
                pl.BlockSpec((None, tok, block), lambda j, *_: (1, 0, j)),
                specs[2],
            ],
            out_specs=pl.BlockSpec(shape[:2] + (1,) + shape[3:], lambda j, *_: (0, 0, j, 0, 0)),
            scratch_shapes=[pltpu.VMEM((shape[1], block, block), F32)],
        ),
        out_shape=jax.ShapeDtypeStruct(shape, BF16),
        compiler_params=params(),
        cost_estimate=COST,
    )(pos, *mine, *other)


def assemble(pos, pieces, refs, w_ref, k):
    for (masks, _), ref in zip(pieces, refs):
        for i, m in enumerate(masks):
            w_ref[k, pos ^ m] = ref[i, k, 0]
    shards, rows, block = w_ref.shape[1:]
    return w_ref[k].reshape(shards * rows, block)


def piece_specs(pieces, first, n_levels, start=0):
    return [
        pl.BlockSpec(
            tuple(map(pl.Element, (p.shape[0], n_levels, 1, p.shape[3], p.shape[4]))),
            lambda j, *_: (0, first, j + start, 0, 0),
        )
        for _, p in pieces
    ]


def w_scratch(pieces, n_levels, shards):
    return pltpu.VMEM((n_levels, shards) + pieces[0][1].shape[3:], BF16)


def rows_kernel(
    pieces, distances, parts, pos_ref, hid_ref, cot_ref, fac_ref, back_ref, left_ref, right_ref,
    *refs
):
    n_cross = len(parts[0][1])
    n_src = n_cross * len(parts)
    w_refs = refs[n_src : n_src + len(pieces)]
    mixed_ref, grad_ref, w_ref = refs[n_src + len(pieces) :][:3]
    block = cot_ref.shape[1]
    j = pl.program_id(0)
    pos = pos_ref[0]
    sources = join(j, parts, refs[:n_src], refs[-n_cross:])

    @pl.when(j == 0)
    def _():
        grad_ref[...] = jnp.zeros_like(grad_ref)

    cot = cot_ref[...]
    mixed = jnp.dot(fac_ref[...], right_ref[...], preferred_element_type=F32)
    for k, distance in enumerate(distances):
        weight = assemble(pos, pieces, w_refs, w_ref, k)
        there = aligned(j ^ distance, block)
        mixed += jnp.dot(hid_ref[:, there], weight, preferred_element_type=F32)
        term = lax.dot_general(cot, weight, NT, preferred_element_type=F32)
        if distance == 0:
            term += lax.dot_general(back_ref[...], left_ref[...], NT, preferred_element_type=F32)
        grad_ref[:, there] += term
    for k, source in enumerate(sources, len(distances)):
        weight = assemble(pos, pieces, w_refs, w_ref, k)
        mixed += jnp.dot(source[:, aligned(j, block)], weight, preferred_element_type=F32)
    mixed_ref[...] = mixed.astype(BF16)


def rows_terms(pos, hidden, cot, factor, back, low_left, low_right, parts, pieces, distances, n_blocks, shards):
    tok, ff = hidden.shape
    block = ff // n_blocks
    rank = factor.shape[1]
    n_cross = len(parts[0][1])
    n_levels = len(distances) + n_cross
    column = pl.BlockSpec((tok, block), lambda j, *_: (0, j))
    whole = pl.BlockSpec((tok, ff), lambda j, *_: (0, 0))
    low = pl.BlockSpec((tok, rank), lambda j, *_: (0, 0))
    sources = [value for _, part in parts for value in part]
    return pl.pallas_call(
        functools.partial(rows_kernel, pieces, distances, parts),
        grid_spec=pltpu.PrefetchScalarGridSpec(
            num_scalar_prefetch=1,
            grid=(n_blocks,),
            in_specs=[
                whole,
                column,
                low,
                low,
                pl.BlockSpec((block, rank), lambda j, *_: (j, 0)),
                pl.BlockSpec((rank, block), lambda j, *_: (0, j)),
            ]
            + [pl.BlockSpec(s.shape, lambda j, *_: (0, 0)) for s in sources]
            + piece_specs(pieces, 0, n_levels),
            out_specs=[column, whole],
            scratch_shapes=[w_scratch(pieces, n_levels, shards)]
            + [pltpu.VMEM((tok, ff), BF16)] * n_cross,
        ),
        out_shape=[jax.ShapeDtypeStruct((tok, ff), BF16), jax.ShapeDtypeStruct((tok, ff), F32)],
        compiler_params=params(),
        cost_estimate=COST,
    )(pos, hidden, cot, factor, back, low_left, low_right, *sources, *[p for _, p in pieces])


def back_kernel(pieces, n_levels, pos_ref, cot_ref, *refs):
    w_refs, (out_refs, w_ref) = refs[: len(pieces)], (refs[len(pieces) : -1], refs[-1])
    for k in range(n_levels):
        weight = assemble(pos_ref[0], pieces, w_refs, w_ref, k)
        term = lax.dot_general(cot_ref[...], weight, NT, preferred_element_type=F32)
        out_refs[k][...] = term.astype(BF16)


def back_terms(pos, cot, pieces, first, n_levels, shards, start, count):
    tok = cot.shape[0]
    block = pieces[0][1].shape[-1]
    column = pl.BlockSpec((tok, block), lambda j, *_: (0, j))
    return pl.pallas_call(
        functools.partial(back_kernel, pieces, n_levels),
        grid_spec=pltpu.PrefetchScalarGridSpec(
            num_scalar_prefetch=1,
            grid=(count,),
            in_specs=[pl.BlockSpec((tok, block), lambda j, *_: (0, j + start))]
            + piece_specs(pieces, first, n_levels, start),
            out_specs=[column] * n_levels,
            scratch_shapes=[w_scratch(pieces, n_levels, shards)],
        ),
        out_shape=[jax.ShapeDtypeStruct((tok, count * block), BF16)] * n_levels,
        compiler_params=params(),
        cost_estimate=COST,
    )(pos, cot, *[p for _, p in pieces])


def highest(mask):
    return 1 << mask.bit_length() - 1


def gather_pieces(own, shards, tie):
    half = own.shape[-1] // 2
    low, high, full = slice(0, half), slice(half, None), slice(None)
    far = {0: [(full, own)]}
    for mask in range(2, shards, 2):
        last_a, last_b = highest(mask), mask & -mask
        if last_a == last_b:
            far[mask] = [(full, swap(own, "dp", mask))]
            continue
        far[mask] = []
        for last, columns in ((last_a, low), (last_b, high)):
            for held, value in far[mask ^ last]:
                if held == full:
                    value = value[..., columns]
                elif held != columns:
                    continue
                far[mask].append((columns, swap(after(value, *tie), "dp", last)))
    near = [mask for mask in far if len(far[mask]) == 1]
    rest = [mask for mask in far if mask not in near]
    pieces = [(near, jnp.stack([far[mask][0][1] for mask in near]))]
    if rest:
        joined = [jnp.concatenate([value for _, value in far[mask]], axis=-1) for mask in rest]
        pieces.append((rest, jnp.stack(joined)))
    return pieces, [value for mask in far for _, value in far[mask]]


def with_pair(pieces, *ties):
    return pieces + [
        ([mask | 1 for mask in masks], swap(after(value, *tie), "dp", 1))
        for (masks, value), tie in zip(pieces, ties)
    ]


def scatter_sum(parts, shards, *ties):
    half = parts[0].shape[-1] // 2
    bits = list(range(shards.bit_length() - 2))
    totals, received = [], []
    for columns, order in ((slice(0, half), bits), (slice(half, None), bits[::-1])):
        terms = {
            q: [part[q][..., columns] for part in parts] for q in range(shards // 2)
        }
        for step, bit in enumerate(order):
            going = [q for q in sorted(terms) if q >> bit & 1]
            total = jnp.stack([sum(t.astype(F32) for t in terms[q]).astype(BF16) for q in going])
            if step < len(ties):
                total = after(total, *ties[step])
            got = swap(total, "dp", 2 << bit)
            terms = {q: terms[q] for q in terms if not q >> bit & 1}
            for place, q in enumerate(going):
                terms[q ^ 1 << bit] = terms[q ^ 1 << bit] + [got[place]]
        received.append(terms[0][-1])
        totals.append(sum(t.astype(F32) for t in terms[0]))
    return totals, received


def scatter_and_gather(parts, rows, tie, last_tie):
    half = parts[0].shape[-1] // 2
    columns = slice(0, half), slice(half, None)
    shape = parts[0].shape[1:-1] + (half,)
    halves = jnp.stack([rows[..., c] for c in columns])

    def split(parts):
        return [[[part[q][..., c] for part in parts] for q in range(4)] for c in columns]

    terms = split(parts)

    def total(values):
        return sum(v.astype(F32) for v in values).astype(BF16)

    got = []
    for way in range(2):
        going = jnp.concatenate([total(terms[way][q]) for q in (1 + way, 3)] + [halves])
        got.append(swap(after(going, *tie), "dp", 2 << way))
    levels = shape[0]
    terms = split([after(part, *got) for part in parts])
    far, totals = [], []
    for way in range(2):
        mine, ours = got[way][:levels], got[way][levels : 2 * levels]
        passed = got[way][2 * levels :][way : way + 1]
        going = jnp.concatenate([total(terms[way][2 - way] + [ours]), passed])
        last = swap(after(going, *got, *last_tie), "dp", 4 >> way)
        totals.append(sum(v.astype(F32) for v in terms[way][0] + [mine, last[:levels]]))
        far.append(last[levels])
    near = [jnp.concatenate([g[2 * levels], g[2 * levels + 1]], axis=-1) for g in got]
    held = jnp.stack([rows, *near, jnp.concatenate(far, axis=-1)])[:, None]
    return totals, [([0, 2, 4, 6], held), ([1, 3, 5, 7], swap(held, "dp", 1))]


def low_kernel(pieces, pos_ref, *refs):
    w_refs, (left_ref, right_ref, w_ref) = refs[: len(pieces)], refs[len(pieces) :]
    shards, rows, block = w_ref.shape[1:]
    rank = left_ref.shape[1]
    for b in range(w_ref.shape[0]):
        for (masks, _), ref in zip(pieces, w_refs):
            for i, m in enumerate(masks):
                w_ref[b, pos_ref[0] ^ m] = ref[i, 0, b]
        values = w_ref[b].reshape(shards * rows, block).astype(F32)
        there = pl.ds(b * block, block)
        left_ref[there, :] = values[:, :rank]
        right_ref[:, there] = values[:, rank:].T


def low_grads(pos, pieces, shards, rank):
    n_blocks, rows, block = pieces[0][1].shape[2:]
    width = min(4, n_blocks)
    ff = n_blocks * block
    return pl.pallas_call(
        functools.partial(low_kernel, pieces),
        grid_spec=pltpu.PrefetchScalarGridSpec(
            num_scalar_prefetch=1,
            grid=(n_blocks // width,),
            in_specs=[
                pl.BlockSpec((p.shape[0], 1, width, rows, block), lambda j, *_: (0, 0, j, 0, 0))
                for _, p in pieces
            ],
            out_specs=[
                pl.BlockSpec((width * block, rank), lambda j, *_: (j, 0)),
                pl.BlockSpec((rank, width * block), lambda j, *_: (0, j)),
            ],
            scratch_shapes=[pltpu.VMEM((width, shards, rows, block), BF16)],
        ),
        out_shape=[jax.ShapeDtypeStruct((ff, rank), F32), jax.ShapeDtypeStruct((rank, ff), F32)],
        compiler_params=params(),
        cost_estimate=COST,
    )(pos, *[p for _, p in pieces])


def gather_rows(value, shards):
    pos = lax.axis_index("dp")
    for bit in range(shards.bit_length() - 1)[::-1]:
        other = swap(value, "dp", 1 << bit)
        first = pos >> bit & 1 == 0
        pair = jnp.where(first, value, other), jnp.where(first, other, value)
        value = jnp.stack(pair, axis=shards.bit_length() - 1 - bit)
    return value


def per_device(hidden, cotangent, blocks, low_left, low_right):
    tok, ff = hidden.shape
    n_blocks, block = blocks.shape[1], blocks.shape[3]
    shards = lax.axis_size("dp")
    local_bits = n_blocks.bit_length() - 1
    cross_bits = lax.axis_size("tensor").bit_length() - 1
    n_local = 1 + local_bits
    scale = 1.0 / (tok * shards) ** 0.5
    pos = lax.axis_index("dp").astype(jnp.int32).reshape(1)

    factors = jnp.concatenate(
        [
            jnp.dot(hidden, low_left, preferred_element_type=F32),
            lax.dot_general(cotangent, low_right, NT, preferred_element_type=F32),
        ],
        axis=1,
    ).astype(BF16)
    rank = low_left.shape[1]

    def add(value, other):
        return (value.astype(F32) + other.astype(F32)).astype(BF16)

    cuts = [ff * quarter // 4 for quarter in range(5)]
    both = swap(after(jnp.stack([hidden, cotangent]), factors), "dp", 1)
    remote, ready = [], []
    for number, (start, stop) in enumerate(zip(cuts, cuts[1:])):
        part = after(hidden[:, start:stop], *ready, *([both] if ready else []))
        ready = [
            swap(
                jnp.concatenate([part, factors], axis=1) if bit == number < 2 else part,
                "tensor",
                1 << bit,
            )
            for bit in range(cross_bits)
        ]
        remote.append((stop - start, ready))
        if number < 2:
            factors = add(factors, ready[number][:, stop - start :])
        if number == 1:
            for bit in range(2, cross_bits):
                factors = add(factors, swap(factors, "tensor", 1 << bit))
    factor, back = factors[:, :rank], factors[:, rank:]

    pieces, gathered = gather_pieces(blocks, shards, remote[0][1] + remote[1][1])
    direct = gathered[1:3]
    distances = [0] + [1 << level for level in range(local_bits)]
    their_factors = swap(after(factors, *direct, *remote[1][1]), "dp", 1)
    kept = pair_grads(
        pos, (hidden, cotangent, factors), (both, both, their_factors), distances, n_blocks,
        shards, scale,
    )

    pieces = with_pair(pieces, [their_factors], remote[2][1] + [kept])
    cuts = [0, max(1, n_blocks * 7 // 16), max(2, n_blocks * 3 // 4), n_blocks]
    sent, returned, ready = [], [], remote[-1][1]
    for number, (start, stop) in enumerate(zip(cuts, cuts[1:])):
        terms = back_terms(
            pos, cotangent, pieces, n_local,
            cross_bits, shards, start, stop - start,
        )
        ready = [swap(after(t, *ready), "tensor", 1 << bit) for bit, t in enumerate(terms)]
        sent.append(list(terms))
        returned.append(ready)
    keep, send = block_grads(pos, after(cotangent, *sent[0]), remote, n_blocks, shards, scale)
    crossed = swap(send, "dp", 1)
    grads_local, received = scatter_sum(
        [kept], shards, gathered + remote[3][1] + sent[0], returned[0] + sent[1] + [keep]
    )
    mixed_rows, grad_in = rows_terms(
        pos, hidden, after(cotangent, *returned[0], crossed), factor, back, low_left, low_right, remote,
        pieces, distances, n_blocks, shards,
    )

    low = jnp.concatenate([part[n_local] for part in grads_local], axis=-1).astype(BF16)
    tie = received + returned[1] + sent[2] + [mixed_rows]
    if shards == 8:
        grads_cross, low_pieces = scatter_and_gather([keep, crossed], low, tie, returned[2])
        grad_left, grad_right = low_grads(pos, low_pieces, shards, rank)
    else:
        grads_cross, _ = scatter_sum([keep, crossed], shards, tie)
        low = gather_rows(low, shards).reshape(ff, 2 * rank).astype(F32)
        grad_left, grad_right = low[:, :rank], low[:, rank:].T
    grad_blocks = jnp.concatenate(
        [
            jnp.concatenate([a[:n_local], b], axis=0)
            for a, b in zip(grads_local, grads_cross)
        ],
        axis=-1,
    )

    returned = [jnp.concatenate(pair, axis=1) for pair in zip(*returned)]
    grad_hidden = (grad_in + sum(term.astype(F32) for term in returned)).astype(BF16)
    return (mixed_rows, grad_hidden, grad_blocks, grad_left, grad_right)


def solution(mesh):
    placed = (
        P("dp", "tensor"),
        P("dp", "tensor"),
        P(None, "tensor", "dp", None),
        P("tensor", None),
        P(None, "tensor"),
    )
    return jax.shard_map(
        per_device, mesh=mesh, in_specs=placed, out_specs=placed, check_vma=False
    )
```

```python
import functools

import jax
import jax.numpy as jnp
from jax import lax
from jax.experimental import pallas as pl
from jax.experimental.pallas import tpu as pltpu
from jax.sharding import PartitionSpec as P

F32 = jnp.float32
BF16 = jnp.bfloat16
COST = pl.CostEstimate(flops=1, bytes_accessed=1, transcendentals=0)
VMEM_LIMIT = 20 * 1024 * 1024


def swap(value, axis, mask):
    return lax.ppermute(value, axis, [(i, i ^ mask) for i in range(lax.axis_size(axis))])


def params():
    return pltpu.CompilerParams(
        dimension_semantics=("arbitrary",), vmem_limit_bytes=VMEM_LIMIT
    )


def aligned(index, size):
    return pl.ds(pl.multiple_of(index * size, size), size)


TN = (((0,), (0,)), ((), ()))
NT = (((1,), (1,)), ((), ()))


def after(value, *others):
    return lax.optimization_barrier((value, *others))[0]


def join(j, parts, refs, joined):
    @pl.when(j == 0)
    def _():
        places = iter(refs)
        start = 0
        for width, _ in parts:
            for to in joined:
                to[:, start : start + width] = next(places)[:, :width]
            start += width

    return joined


def grads_kernel(n_parts, n_levels, shards, scale, pos_ref, *refs):
    cots, sources = refs[:n_parts], refs[n_parts:-3]
    keep_ref, send_ref, tmp_ref = refs[-3:]
    rows = cots[0].shape[1] // shards
    pos = pos_ref[0]
    for p, cot_ref in enumerate(cots):
        for k in range(n_levels):
            values = sources[p * n_levels + k][...]
            term = lax.dot_general(values, cot_ref[...], TN, preferred_element_type=F32)
            tmp_ref[p, k] = term * scale
            for m in range(shards):
                part = tmp_ref[p, k, aligned(pos ^ m, rows), :].astype(BF16)
                (send_ref if m & 1 else keep_ref)[m >> 1, k, p, 0] = part


def block_grads(pos, cot, parts, n_blocks, shards, scale):
    tok, ff = cot.shape
    block = ff // n_blocks
    rows = block // shards
    n_parts, n_levels = len(parts), len(parts[0][1])
    steps = n_blocks // n_parts
    part = jax.ShapeDtypeStruct((shards // 2, n_levels, n_parts, steps, rows, block), BF16)
    part_spec = pl.BlockSpec(
        (shards // 2, n_levels, n_parts, 1, rows, block), lambda j, *_: (0, 0, 0, j, 0, 0)
    )
    outs = pl.pallas_call(
        functools.partial(grads_kernel, n_parts, n_levels, shards, scale),
        grid_spec=pltpu.PrefetchScalarGridSpec(
            num_scalar_prefetch=1,
            grid=(steps,),
            in_specs=[
                pl.BlockSpec((tok, block), lambda j, *_, p=p: (0, p * steps + j))
                for p in range(n_parts)
            ]
            + [pl.BlockSpec((tok, block), lambda j, *_: (0, j))] * (n_parts * n_levels),
            out_specs=[part_spec, part_spec],
            scratch_shapes=[pltpu.VMEM((n_parts, n_levels, block, block), F32)],
        ),
        out_shape=[part, part],
        compiler_params=params(),
        cost_estimate=COST,
    )(pos, *[cot] * n_parts, *[value for _, part in parts for value in part])
    return [o.reshape(o.shape[:2] + (n_blocks,) + o.shape[4:]) for o in outs]


def pair_kernel(distances, shards, scale, pos_ref, *refs):
    ins, (keep_ref, tmp_ref) = refs[:-2], refs[-2:]
    pair = ins[: len(ins) // 2], ins[len(ins) // 2 :]
    block = ins[1].shape[1]
    rows = block // shards
    j = pl.program_id(0)
    pos = pos_ref[0]

    def product(left, right):
        return lax.dot_general(left, right, TN, preferred_element_type=F32)

    for k, distance in enumerate((*distances, None)):
        if distance is None:
            rank = ins[2].shape[1] // 2
            tmp_ref[k, :, :rank] = scale * sum(
                product(hid[:, aligned(j, block)], fac[:, rank:]) for hid, _, fac in pair
            )
            tmp_ref[k, :, rank:] = scale * sum(
                product(cot[...], fac[:, :rank]) for _, cot, fac in pair
            )
        else:
            there = aligned(j ^ distance, block)
            tmp_ref[k] = scale * sum(product(hid[:, there], cot[...]) for hid, cot, _ in pair)
        for m in range(0, shards, 2):
            keep_ref[m >> 1, k, 0] = tmp_ref[k, aligned(pos ^ m, rows), :].astype(BF16)


def pair_grads(pos, mine, other, distances, n_blocks, shards, scale):
    tok, ff = mine[0].shape
    block = ff // n_blocks
    shape = (shards // 2, len(distances) + 1, n_blocks, block // shards, block)
    specs = [
        pl.BlockSpec((tok, ff), lambda j, *_: (0, 0)),
        pl.BlockSpec((tok, block), lambda j, *_: (0, j)),
        pl.BlockSpec(mine[2].shape, lambda j, *_: (0, 0)),
    ]
    return pl.pallas_call(
        functools.partial(pair_kernel, distances, shards, scale),
        grid_spec=pltpu.PrefetchScalarGridSpec(
            num_scalar_prefetch=1,
            grid=(n_blocks,),
            in_specs=specs
            + [
                pl.BlockSpec((None, tok, ff), lambda j, *_: (0, 0, 0)),
                pl.BlockSpec((None, tok, block), lambda j, *_: (1, 0, j)),
                specs[2],
            ],
            out_specs=pl.BlockSpec(shape[:2] + (1,) + shape[3:], lambda j, *_: (0, 0, j, 0, 0)),
            scratch_shapes=[pltpu.VMEM((shape[1], block, block), F32)],
        ),
        out_shape=jax.ShapeDtypeStruct(shape, BF16),
        compiler_params=params(),
        cost_estimate=COST,
    )(pos, *mine, *other)


def assemble(pos, pieces, refs, w_ref, k):
    for (masks, _), ref in zip(pieces, refs):
        for i, m in enumerate(masks):
            w_ref[k, pos ^ m] = ref[i, k, 0]
    shards, rows, block = w_ref.shape[1:]
    return w_ref[k].reshape(shards * rows, block)


def piece_specs(pieces, first, n_levels, start=0):
    return [
        pl.BlockSpec(
            tuple(map(pl.Element, (p.shape[0], n_levels, 1, p.shape[3], p.shape[4]))),
            lambda j, *_: (0, first, j + start, 0, 0),
        )
        for _, p in pieces
    ]


def w_scratch(pieces, n_levels, shards):
    return pltpu.VMEM((n_levels, shards) + pieces[0][1].shape[3:], BF16)


def rows_kernel(
    pieces, distances, parts, pos_ref, hid_ref, cot_ref, fac_ref, back_ref, left_ref, right_ref,
    *refs
):
    n_cross = len(parts[0][1])
    n_src = n_cross * len(parts)
    w_refs = refs[n_src : n_src + len(pieces)]
    mixed_ref, grad_ref, w_ref = refs[n_src + len(pieces) :][:3]
    block = cot_ref.shape[1]
    j = pl.program_id(0)
    pos = pos_ref[0]
    sources = join(j, parts, refs[:n_src], refs[-n_cross:])

    @pl.when(j == 0)
    def _():
        grad_ref[...] = jnp.zeros_like(grad_ref)

    cot = cot_ref[...]
    mixed = jnp.dot(fac_ref[...], right_ref[...], preferred_element_type=F32)
    for k, distance in enumerate(distances):
        weight = assemble(pos, pieces, w_refs, w_ref, k)
        there = aligned(j ^ distance, block)
        mixed += jnp.dot(hid_ref[:, there], weight, preferred_element_type=F32)
        term = lax.dot_general(cot, weight, NT, preferred_element_type=F32)
        if distance == 0:
            term += lax.dot_general(back_ref[...], left_ref[...], NT, preferred_element_type=F32)
        grad_ref[:, there] += term
    for k, source in enumerate(sources, len(distances)):
        weight = assemble(pos, pieces, w_refs, w_ref, k)
        mixed += jnp.dot(source[:, aligned(j, block)], weight, preferred_element_type=F32)
    mixed_ref[...] = mixed.astype(BF16)


def rows_terms(pos, hidden, cot, factor, back, low_left, low_right, parts, pieces, distances, n_blocks, shards):
    tok, ff = hidden.shape
    block = ff // n_blocks
    rank = factor.shape[1]
    n_cross = len(parts[0][1])
    n_levels = len(distances) + n_cross
    column = pl.BlockSpec((tok, block), lambda j, *_: (0, j))
    whole = pl.BlockSpec((tok, ff), lambda j, *_: (0, 0))
    low = pl.BlockSpec((tok, rank), lambda j, *_: (0, 0))
    sources = [value for _, part in parts for value in part]
    return pl.pallas_call(
        functools.partial(rows_kernel, pieces, distances, parts),
        grid_spec=pltpu.PrefetchScalarGridSpec(
            num_scalar_prefetch=1,
            grid=(n_blocks,),
            in_specs=[
                whole,
                column,
                low,
                low,
                pl.BlockSpec((block, rank), lambda j, *_: (j, 0)),
                pl.BlockSpec((rank, block), lambda j, *_: (0, j)),
            ]
            + [pl.BlockSpec(s.shape, lambda j, *_: (0, 0)) for s in sources]
            + piece_specs(pieces, 0, n_levels),
            out_specs=[column, whole],
            scratch_shapes=[w_scratch(pieces, n_levels, shards)]
            + [pltpu.VMEM((tok, ff), BF16)] * n_cross,
        ),
        out_shape=[jax.ShapeDtypeStruct((tok, ff), BF16), jax.ShapeDtypeStruct((tok, ff), F32)],
        compiler_params=params(),
        cost_estimate=COST,
    )(pos, hidden, cot, factor, back, low_left, low_right, *sources, *[p for _, p in pieces])


def back_kernel(pieces, n_levels, pos_ref, cot_ref, *refs):
    w_refs, (out_refs, w_ref) = refs[: len(pieces)], (refs[len(pieces) : -1], refs[-1])
    for k in range(n_levels):
        weight = assemble(pos_ref[0], pieces, w_refs, w_ref, k)
        term = lax.dot_general(cot_ref[...], weight, NT, preferred_element_type=F32)
        out_refs[k][...] = term.astype(BF16)


def back_terms(pos, cot, pieces, first, n_levels, shards, start, count):
    tok = cot.shape[0]
    block = pieces[0][1].shape[-1]
    column = pl.BlockSpec((tok, block), lambda j, *_: (0, j))
    return pl.pallas_call(
        functools.partial(back_kernel, pieces, n_levels),
        grid_spec=pltpu.PrefetchScalarGridSpec(
            num_scalar_prefetch=1,
            grid=(count,),
            in_specs=[pl.BlockSpec((tok, block), lambda j, *_: (0, j + start))]
            + piece_specs(pieces, first, n_levels, start),
            out_specs=[column] * n_levels,
            scratch_shapes=[w_scratch(pieces, n_levels, shards)],
        ),
        out_shape=[jax.ShapeDtypeStruct((tok, count * block), BF16)] * n_levels,
        compiler_params=params(),
        cost_estimate=COST,
    )(pos, cot, *[p for _, p in pieces])


def highest(mask):
    return 1 << mask.bit_length() - 1


def gather_pieces(own, shards, tie):
    half = own.shape[-1] // 2
    low, high, full = slice(0, half), slice(half, None), slice(None)
    far, cut = {0: [(full, own)]}, []
    for mask in range(2, shards, 2):
        last_a, last_b = highest(mask), mask & -mask
        if last_a == last_b:
            far[mask] = [(full, swap(own, "dp", mask))]
            continue
        far[mask] = []
        for last, columns in ((last_a, low), (last_b, high)):
            for held, value in far[mask ^ last]:
                if held == full:
                    value = value[..., columns]
                elif held != columns:
                    continue
                value = after(value, *tie)
                cut.append(value)
                far[mask].append((columns, swap(value, "dp", last)))
    near = [mask for mask in far if len(far[mask]) == 1]
    rest = [mask for mask in far if mask not in near]
    pieces = [(near, jnp.stack([after(far[mask][0][1], *cut) for mask in near]))]
    if rest:
        joined = [jnp.concatenate([value for _, value in far[mask]], axis=-1) for mask in rest]
        pieces.append((rest, jnp.stack(joined)))
    return pieces, [value for mask in far for _, value in far[mask]]


def with_pair(pieces, *ties):
    return pieces + [
        ([mask | 1 for mask in masks], swap(after(value, *tie), "dp", 1))
        for (masks, value), tie in zip(pieces, ties)
    ]


def scatter_sum(parts, shards, *ties):
    half = parts[0].shape[-1] // 2
    bits = list(range(shards.bit_length() - 2))
    totals, received = [], []
    for columns, order in ((slice(0, half), bits), (slice(half, None), bits[::-1])):
        terms = {
            q: [part[q][..., columns] for part in parts] for q in range(shards // 2)
        }
        for step, bit in enumerate(order):
            going = [q for q in sorted(terms) if q >> bit & 1]
            total = jnp.stack([sum(t.astype(F32) for t in terms[q]).astype(BF16) for q in going])
            if step < len(ties):
                total = after(total, *ties[step])
            got = swap(total, "dp", 2 << bit)
            terms = {q: terms[q] for q in terms if not q >> bit & 1}
            for place, q in enumerate(going):
                terms[q ^ 1 << bit] = terms[q ^ 1 << bit] + [got[place]]
        received.append(terms[0][-1])
        totals.append(sum(t.astype(F32) for t in terms[0]))
    return totals, received


def scatter_and_gather(parts, rows, tie, last_tie):
    half = parts[0].shape[-1] // 2
    columns = slice(0, half), slice(half, None)
    shape = parts[0].shape[1:-1] + (half,)
    halves = jnp.stack([rows[..., c] for c in columns])

    def split(parts):
        return [[[part[q][..., c] for part in parts] for q in range(4)] for c in columns]

    terms = split(parts)

    def total(values):
        return sum(v.astype(F32) for v in values).astype(BF16)

    got = []
    for way in range(2):
        going = jnp.concatenate([total(terms[way][q]) for q in (1 + way, 3)] + [halves])
        got.append(swap(after(going, *tie), "dp", 2 << way))
    levels = shape[0]
    terms = split([after(part, *got) for part in parts])
    far, totals = [], []
    for way in range(2):
        mine, ours = got[way][:levels], got[way][levels : 2 * levels]
        passed = got[way][2 * levels :][way : way + 1]
        going = jnp.concatenate([total(terms[way][2 - way] + [ours]), passed])
        last = swap(after(going, *got, *last_tie), "dp", 4 >> way)
        totals.append(sum(v.astype(F32) for v in terms[way][0] + [mine, last[:levels]]))
        far.append(last[levels])
    near = [jnp.concatenate([g[2 * levels], g[2 * levels + 1]], axis=-1) for g in got]
    held = jnp.stack([rows, *near, jnp.concatenate(far, axis=-1)])[:, None]
    return totals, [([0, 2, 4, 6], held), ([1, 3, 5, 7], swap(held, "dp", 1))]


def low_kernel(pieces, pos_ref, *refs):
    w_refs, (left_ref, right_ref, w_ref) = refs[: len(pieces)], refs[len(pieces) :]
    shards, rows, block = w_ref.shape[1:]
    rank = left_ref.shape[1]
    for b in range(w_ref.shape[0]):
        for (masks, _), ref in zip(pieces, w_refs):
            for i, m in enumerate(masks):
                w_ref[b, pos_ref[0] ^ m] = ref[i, 0, b]
        values = w_ref[b].reshape(shards * rows, block).astype(F32)
        there = pl.ds(b * block, block)
        left_ref[there, :] = values[:, :rank]
        right_ref[:, there] = values[:, rank:].T


def low_grads(pos, pieces, shards, rank):
    n_blocks, rows, block = pieces[0][1].shape[2:]
    width = min(4, n_blocks)
    ff = n_blocks * block
    return pl.pallas_call(
        functools.partial(low_kernel, pieces),
        grid_spec=pltpu.PrefetchScalarGridSpec(
            num_scalar_prefetch=1,
            grid=(n_blocks // width,),
            in_specs=[
                pl.BlockSpec((p.shape[0], 1, width, rows, block), lambda j, *_: (0, 0, j, 0, 0))
                for _, p in pieces
            ],
            out_specs=[
                pl.BlockSpec((width * block, rank), lambda j, *_: (j, 0)),
                pl.BlockSpec((rank, width * block), lambda j, *_: (0, j)),
            ],
            scratch_shapes=[pltpu.VMEM((width, shards, rows, block), BF16)],
        ),
        out_shape=[jax.ShapeDtypeStruct((ff, rank), F32), jax.ShapeDtypeStruct((rank, ff), F32)],
        compiler_params=params(),
        cost_estimate=COST,
    )(pos, *[p for _, p in pieces])


def gather_rows(value, shards):
    pos = lax.axis_index("dp")
    for bit in range(shards.bit_length() - 1)[::-1]:
        other = swap(value, "dp", 1 << bit)
        first = pos >> bit & 1 == 0
        pair = jnp.where(first, value, other), jnp.where(first, other, value)
        value = jnp.stack(pair, axis=shards.bit_length() - 1 - bit)
    return value


def per_device(hidden, cotangent, blocks, low_left, low_right):
    tok, ff = hidden.shape
    n_blocks, block = blocks.shape[1], blocks.shape[3]
    shards = lax.axis_size("dp")
    local_bits = n_blocks.bit_length() - 1
    cross_bits = lax.axis_size("tensor").bit_length() - 1
    n_local = 1 + local_bits
    scale = 1.0 / (tok * shards) ** 0.5
    pos = lax.axis_index("dp").astype(jnp.int32).reshape(1)

    factors = jnp.concatenate(
        [
            jnp.dot(hidden, low_left, preferred_element_type=F32),
            lax.dot_general(cotangent, low_right, NT, preferred_element_type=F32),
        ],
        axis=1,
    ).astype(BF16)
    rank = low_left.shape[1]

    def add(value, other):
        return (value.astype(F32) + other.astype(F32)).astype(BF16)

    cuts = [ff * quarter // 4 for quarter in range(5)]
    both = swap(after(jnp.stack([hidden, cotangent]), factors), "dp", 1)
    remote, ready = [], []
    for number, (start, stop) in enumerate(zip(cuts, cuts[1:])):
        part = after(hidden[:, start:stop], *ready, *([both] if ready else []))
        ready = [
            swap(
                jnp.concatenate([part, factors], axis=1) if bit == number < 2 else part,
                "tensor",
                1 << bit,
            )
            for bit in range(cross_bits)
        ]
        remote.append((stop - start, ready))
        if number < 2:
            factors = add(factors, ready[number][:, stop - start :])
        if number == 1:
            for bit in range(2, cross_bits):
                factors = add(factors, swap(factors, "tensor", 1 << bit))
    factor, back = factors[:, :rank], factors[:, rank:]

    pieces, gathered = gather_pieces(blocks, shards, remote[0][1] + remote[1][1])
    direct = gathered[1:3]
    distances = [0] + [1 << level for level in range(local_bits)]
    their_factors = swap(after(factors, *direct, *remote[1][1]), "dp", 1)
    kept = pair_grads(
        pos, (hidden, cotangent, factors), (both, both, their_factors), distances, n_blocks,
        shards, scale,
    )

    pieces = with_pair(pieces, [their_factors], remote[2][1] + [kept])
    cuts = [0, max(1, n_blocks * 7 // 16), max(2, n_blocks * 3 // 4), n_blocks]
    sent, returned, ready = [], [], remote[-1][1]
    for number, (start, stop) in enumerate(zip(cuts, cuts[1:])):
        terms = back_terms(
            pos, cotangent, pieces, n_local,
            cross_bits, shards, start, stop - start,
        )
        ready = [swap(after(t, *ready), "tensor", 1 << bit) for bit, t in enumerate(terms)]
        sent.append(list(terms))
        returned.append(ready)
    keep, send = block_grads(pos, after(cotangent, *sent[0]), remote, n_blocks, shards, scale)
    crossed = swap(send, "dp", 1)
    grads_local, received = scatter_sum(
        [kept], shards, gathered + remote[3][1] + sent[0], returned[0] + sent[1] + [keep]
    )
    mixed_rows, grad_in = rows_terms(
        pos, hidden, after(cotangent, *returned[0], crossed), factor, back, low_left, low_right, remote,
        pieces, distances, n_blocks, shards,
    )

    low = jnp.concatenate([part[n_local] for part in grads_local], axis=-1).astype(BF16)
    tie = received + returned[1] + sent[2] + [mixed_rows]
    if shards == 8:
        grads_cross, low_pieces = scatter_and_gather([keep, crossed], low, tie, returned[2])
        grad_left, grad_right = low_grads(pos, low_pieces, shards, rank)
    else:
        grads_cross, _ = scatter_sum([keep, crossed], shards, tie)
        low = gather_rows(low, shards).reshape(ff, 2 * rank).astype(F32)
        grad_left, grad_right = low[:, :rank], low[:, rank:].T
    grad_blocks = jnp.concatenate(
        [
            jnp.concatenate([a[:n_local], b], axis=0)
            for a, b in zip(grads_local, grads_cross)
        ],
        axis=-1,
    )

    returned = [jnp.concatenate(pair, axis=1) for pair in zip(*returned)]
    grad_hidden = (grad_in + sum(term.astype(F32) for term in returned)).astype(BF16)
    return (mixed_rows, grad_hidden, grad_blocks, grad_left, grad_right)


def solution(mesh):
    placed = (
        P("dp", "tensor"),
        P("dp", "tensor"),
        P(None, "tensor", "dp", None),
        P("tensor", None),
        P(None, "tensor"),
    )
    return jax.shard_map(
        per_device, mesh=mesh, in_specs=placed, out_specs=placed, check_vma=False
    )
```

```python
import functools

import jax
import jax.numpy as jnp
from jax import lax
from jax.experimental import pallas as pl
from jax.experimental.pallas import tpu as pltpu
from jax.sharding import PartitionSpec as P

F32 = jnp.float32
BF16 = jnp.bfloat16
COST = pl.CostEstimate(flops=1, bytes_accessed=1, transcendentals=0)
VMEM_LIMIT = 16 * 1024 * 1024


def swap(value, axis, mask):
    return lax.ppermute(value, axis, [(i, i ^ mask) for i in range(lax.axis_size(axis))])


def params():
    return pltpu.CompilerParams(
        dimension_semantics=("arbitrary",), vmem_limit_bytes=VMEM_LIMIT
    )


def aligned(index, size):
    return pl.ds(pl.multiple_of(index * size, size), size)


TN = (((0,), (0,)), ((), ()))
NT = (((1,), (1,)), ((), ()))


def after(value, *others):
    return lax.optimization_barrier((value, *others))[0]


def join(j, parts, refs, joined):
    @pl.when(j == 0)
    def _():
        places = iter(refs)
        start = 0
        for width, _ in parts:
            for to in joined:
                to[:, start : start + width] = next(places)[:, :width]
            start += width

    return joined


def grads_kernel(n_parts, n_levels, shards, scale, pos_ref, *refs):
    cots, sources = refs[:n_parts], refs[n_parts:-3]
    keep_ref, send_ref, tmp_ref = refs[-3:]
    rows = cots[0].shape[1] // shards
    pos = pos_ref[0]
    for p, cot_ref in enumerate(cots):
        for k in range(n_levels):
            values = sources[p * n_levels + k][...]
            term = lax.dot_general(values, cot_ref[...], TN, preferred_element_type=F32)
            tmp_ref[p, k] = term * scale
            for m in range(shards):
                part = tmp_ref[p, k, aligned(pos ^ m, rows), :].astype(BF16)
                (send_ref if m & 1 else keep_ref)[m >> 1, k, p, 0] = part


def block_grads(pos, cot, parts, n_blocks, shards, scale):
    tok, ff = cot.shape
    block = ff // n_blocks
    rows = block // shards
    n_parts, n_levels = len(parts), len(parts[0][1])
    steps = n_blocks // n_parts
    part = jax.ShapeDtypeStruct((shards // 2, n_levels, n_parts, steps, rows, block), BF16)
    part_spec = pl.BlockSpec(
        (shards // 2, n_levels, n_parts, 1, rows, block), lambda j, *_: (0, 0, 0, j, 0, 0)
    )
    outs = pl.pallas_call(
        functools.partial(grads_kernel, n_parts, n_levels, shards, scale),
        grid_spec=pltpu.PrefetchScalarGridSpec(
            num_scalar_prefetch=1,
            grid=(steps,),
            in_specs=[
                pl.BlockSpec((tok, block), lambda j, *_, p=p: (0, p * steps + j))
                for p in range(n_parts)
            ]
            + [pl.BlockSpec((tok, block), lambda j, *_: (0, j))] * (n_parts * n_levels),
            out_specs=[part_spec, part_spec],
            scratch_shapes=[pltpu.VMEM((n_parts, n_levels, block, block), F32)],
        ),
        out_shape=[part, part],
        compiler_params=params(),
        cost_estimate=COST,
    )(pos, *[cot] * n_parts, *[value for _, part in parts for value in part])
    return [o.reshape(o.shape[:2] + (n_blocks,) + o.shape[4:]) for o in outs]


def pair_kernel(distances, shards, scale, pos_ref, *refs):
    ins, (keep_ref, tmp_ref) = refs[:-2], refs[-2:]
    pair = ins[: len(ins) // 2], ins[len(ins) // 2 :]
    block = ins[1].shape[1]
    rows = block // shards
    j = pl.program_id(0)
    pos = pos_ref[0]

    def product(left, right):
        return lax.dot_general(left, right, TN, preferred_element_type=F32)

    for k, distance in enumerate((*distances, None)):
        if distance is None:
            rank = ins[2].shape[1] // 2
            tmp_ref[k, :, :rank] = scale * sum(
                product(hid[:, aligned(j, block)], fac[:, rank:]) for hid, _, fac in pair
            )
            tmp_ref[k, :, rank:] = scale * sum(
                product(cot[...], fac[:, :rank]) for _, cot, fac in pair
            )
        else:
            there = aligned(j ^ distance, block)
            tmp_ref[k] = scale * sum(product(hid[:, there], cot[...]) for hid, cot, _ in pair)
        for m in range(0, shards, 2):
            keep_ref[m >> 1, k, 0] = tmp_ref[k, aligned(pos ^ m, rows), :].astype(BF16)


def pair_grads(pos, mine, other, distances, n_blocks, shards, scale):
    tok, ff = mine[0].shape
    block = ff // n_blocks
    shape = (shards // 2, len(distances) + 1, n_blocks, block // shards, block)
    specs = [
        pl.BlockSpec((tok, ff), lambda j, *_: (0, 0)),
        pl.BlockSpec((tok, block), lambda j, *_: (0, j)),
        pl.BlockSpec(mine[2].shape, lambda j, *_: (0, 0)),
    ]
    return pl.pallas_call(
        functools.partial(pair_kernel, distances, shards, scale),
        grid_spec=pltpu.PrefetchScalarGridSpec(
            num_scalar_prefetch=1,
            grid=(n_blocks,),
            in_specs=specs
            + [
                pl.BlockSpec((None, tok, ff), lambda j, *_: (0, 0, 0)),
                pl.BlockSpec((None, tok, block), lambda j, *_: (1, 0, j)),
                specs[2],
            ],
            out_specs=pl.BlockSpec(shape[:2] + (1,) + shape[3:], lambda j, *_: (0, 0, j, 0, 0)),
            scratch_shapes=[pltpu.VMEM((shape[1], block, block), F32)],
        ),
        out_shape=jax.ShapeDtypeStruct(shape, BF16),
        compiler_params=params(),
        cost_estimate=COST,
    )(pos, *mine, *other)


def assemble(pos, pieces, refs, w_ref, k):
    for (masks, _), ref in zip(pieces, refs):
        for i, m in enumerate(masks):
            w_ref[k, pos ^ m] = ref[i, k, 0]
    shards, rows, block = w_ref.shape[1:]
    return w_ref[k].reshape(shards * rows, block)


def piece_specs(pieces, first, n_levels, start=0):
    return [
        pl.BlockSpec(
            tuple(map(pl.Element, (p.shape[0], n_levels, 1, p.shape[3], p.shape[4]))),
            lambda j, *_: (0, first, j + start, 0, 0),
        )
        for _, p in pieces
    ]


def w_scratch(pieces, n_levels, shards):
    return pltpu.VMEM((n_levels, shards) + pieces[0][1].shape[3:], BF16)


def rows_kernel(
    pieces, distances, parts, pos_ref, hid_ref, cot_ref, fac_ref, back_ref, left_ref, right_ref,
    *refs
):
    n_cross = len(parts[0][1])
    n_src = n_cross * len(parts)
    w_refs = refs[n_src : n_src + len(pieces)]
    mixed_ref, grad_ref, w_ref = refs[n_src + len(pieces) :][:3]
    block = cot_ref.shape[1]
    j = pl.program_id(0)
    pos = pos_ref[0]
    sources = join(j, parts, refs[:n_src], refs[-n_cross:])

    @pl.when(j == 0)
    def _():
        grad_ref[...] = jnp.zeros_like(grad_ref)

    cot = cot_ref[...]
    mixed = jnp.dot(fac_ref[...], right_ref[...], preferred_element_type=F32)
    for k, distance in enumerate(distances):
        weight = assemble(pos, pieces, w_refs, w_ref, k)
        there = aligned(j ^ distance, block)
        mixed += jnp.dot(hid_ref[:, there], weight, preferred_element_type=F32)
        term = lax.dot_general(cot, weight, NT, preferred_element_type=F32)
        if distance == 0:
            term += lax.dot_general(back_ref[...], left_ref[...], NT, preferred_element_type=F32)
        grad_ref[:, there] += term
    for k, source in enumerate(sources, len(distances)):
        weight = assemble(pos, pieces, w_refs, w_ref, k)
        mixed += jnp.dot(source[:, aligned(j, block)], weight, preferred_element_type=F32)
    mixed_ref[...] = mixed.astype(BF16)


def rows_terms(pos, hidden, cot, factor, back, low_left, low_right, parts, pieces, distances, n_blocks, shards):
    tok, ff = hidden.shape
    block = ff // n_blocks
    rank = factor.shape[1]
    n_cross = len(parts[0][1])
    n_levels = len(distances) + n_cross
    column = pl.BlockSpec((tok, block), lambda j, *_: (0, j))
    whole = pl.BlockSpec((tok, ff), lambda j, *_: (0, 0))
    low = pl.BlockSpec((tok, rank), lambda j, *_: (0, 0))
    sources = [value for _, part in parts for value in part]
    return pl.pallas_call(
        functools.partial(rows_kernel, pieces, distances, parts),
        grid_spec=pltpu.PrefetchScalarGridSpec(
            num_scalar_prefetch=1,
            grid=(n_blocks,),
            in_specs=[
                pl.BlockSpec((tok, ff), lambda j, *_: (0, 0), pipeline_mode=pl.Buffered(1)),
                column,
                low,
                low,
                pl.BlockSpec((block, rank), lambda j, *_: (j, 0)),
                pl.BlockSpec((rank, block), lambda j, *_: (0, j)),
            ]
            + [
                pl.BlockSpec(s.shape, lambda j, *_: (0, 0), pipeline_mode=pl.Buffered(1))
                for s in sources
            ]
            + piece_specs(pieces, 0, n_levels),
            out_specs=[column, whole],
            scratch_shapes=[w_scratch(pieces, n_levels, shards)]
            + [pltpu.VMEM((tok, ff), BF16)] * n_cross,
        ),
        out_shape=[jax.ShapeDtypeStruct((tok, ff), BF16), jax.ShapeDtypeStruct((tok, ff), F32)],
        compiler_params=params(),
        cost_estimate=COST,
    )(pos, hidden, cot, factor, back, low_left, low_right, *sources, *[p for _, p in pieces])


def back_kernel(pieces, n_levels, pos_ref, cot_ref, *refs):
    w_refs, (out_refs, w_ref) = refs[: len(pieces)], (refs[len(pieces) : -1], refs[-1])
    for k in range(n_levels):
        weight = assemble(pos_ref[0], pieces, w_refs, w_ref, k)
        term = lax.dot_general(cot_ref[...], weight, NT, preferred_element_type=F32)
        out_refs[k][...] = term.astype(BF16)


def back_terms(pos, cot, pieces, first, n_levels, shards, start, count):
    tok = cot.shape[0]
    block = pieces[0][1].shape[-1]
    column = pl.BlockSpec((tok, block), lambda j, *_: (0, j))
    return pl.pallas_call(
        functools.partial(back_kernel, pieces, n_levels),
        grid_spec=pltpu.PrefetchScalarGridSpec(
            num_scalar_prefetch=1,
            grid=(count,),
            in_specs=[pl.BlockSpec((tok, block), lambda j, *_: (0, j + start))]
            + piece_specs(pieces, first, n_levels, start),
            out_specs=[column] * n_levels,
            scratch_shapes=[w_scratch(pieces, n_levels, shards)],
        ),
        out_shape=[jax.ShapeDtypeStruct((tok, count * block), BF16)] * n_levels,
        compiler_params=params(),
        cost_estimate=COST,
    )(pos, cot, *[p for _, p in pieces])


def highest(mask):
    return 1 << mask.bit_length() - 1


def gather_pieces(own, shards, tie):
    half = own.shape[-1] // 2
    low, high, full = slice(0, half), slice(half, None), slice(None)
    far, cut = {0: [(full, own)]}, []
    for mask in range(2, shards, 2):
        last_a, last_b = highest(mask), mask & -mask
        if last_a == last_b:
            far[mask] = [(full, swap(own, "dp", mask))]
            continue
        far[mask] = []
        for last, columns in ((last_a, low), (last_b, high)):
            for held, value in far[mask ^ last]:
                if held == full:
                    value = value[..., columns]
                elif held != columns:
                    continue
                value = after(value, *tie)
                cut.append(value)
                far[mask].append((columns, swap(value, "dp", last)))
    near = [mask for mask in far if len(far[mask]) == 1]
    rest = [mask for mask in far if mask not in near]
    pieces = [(near, jnp.stack([after(far[mask][0][1], *cut) for mask in near]))]
    if rest:
        joined = [jnp.concatenate([value for _, value in far[mask]], axis=-1) for mask in rest]
        pieces.append((rest, jnp.stack(joined)))
    return pieces, [value for mask in far for _, value in far[mask]]


def with_pair(pieces, *ties):
    return pieces + [
        ([mask | 1 for mask in masks], swap(after(value, *tie), "dp", 1))
        for (masks, value), tie in zip(pieces, ties)
    ]


def scatter_sum(parts, shards, *ties):
    half = parts[0].shape[-1] // 2
    bits = list(range(shards.bit_length() - 2))
    totals, received = [], []
    for columns, order in ((slice(0, half), bits), (slice(half, None), bits[::-1])):
        terms = {
            q: [part[q][..., columns] for part in parts] for q in range(shards // 2)
        }
        for step, bit in enumerate(order):
            going = [q for q in sorted(terms) if q >> bit & 1]
            total = jnp.stack([sum(t.astype(F32) for t in terms[q]).astype(BF16) for q in going])
            if step < len(ties):
                total = after(total, *ties[step])
            got = swap(total, "dp", 2 << bit)
            terms = {q: terms[q] for q in terms if not q >> bit & 1}
            for place, q in enumerate(going):
                terms[q ^ 1 << bit] = terms[q ^ 1 << bit] + [got[place]]
        received.append(terms[0][-1])
        totals.append(sum(t.astype(F32) for t in terms[0]))
    return totals, received


def scatter_and_gather(parts, rows, tie, last_tie):
    half = parts[0].shape[-1] // 2
    columns = slice(0, half), slice(half, None)
    shape = parts[0].shape[1:-1] + (half,)
    halves = jnp.stack([rows[..., c] for c in columns])

    def split(parts):
        return [[[part[q][..., c] for part in parts] for q in range(4)] for c in columns]

    terms = split(parts)

    def total(values):
        return sum(v.astype(F32) for v in values).astype(BF16)

    got = []
    for way in range(2):
        going = jnp.concatenate([total(terms[way][q]) for q in (1 + way, 3)] + [halves])
        got.append(swap(after(going, *tie), "dp", 2 << way))
    levels = shape[0]
    terms = split([after(part, *got) for part in parts])
    far, totals = [], []
    for way in range(2):
        mine, ours = got[way][:levels], got[way][levels : 2 * levels]
        passed = got[way][2 * levels :][way : way + 1]
        going = jnp.concatenate([total(terms[way][2 - way] + [ours]), passed])
        last = swap(after(going, *got, *last_tie), "dp", 4 >> way)
        totals.append(sum(v.astype(F32) for v in terms[way][0] + [mine, last[:levels]]))
        far.append(last[levels])
    near = [jnp.concatenate([g[2 * levels], g[2 * levels + 1]], axis=-1) for g in got]
    held = jnp.stack([rows, *near, jnp.concatenate(far, axis=-1)])[:, None]
    return totals, [([0, 2, 4, 6], held), ([1, 3, 5, 7], swap(held, "dp", 1))]


def low_kernel(pieces, pos_ref, *refs):
    w_refs, (left_ref, right_ref, w_ref) = refs[: len(pieces)], refs[len(pieces) :]
    shards, rows, block = w_ref.shape[1:]
    rank = left_ref.shape[1]
    for b in range(w_ref.shape[0]):
        for (masks, _), ref in zip(pieces, w_refs):
            for i, m in enumerate(masks):
                w_ref[b, pos_ref[0] ^ m] = ref[i, 0, b]
        values = w_ref[b].reshape(shards * rows, block).astype(F32)
        there = pl.ds(b * block, block)
        left_ref[there, :] = values[:, :rank]
        right_ref[:, there] = values[:, rank:].T


def low_grads(pos, pieces, shards, rank):
    n_blocks, rows, block = pieces[0][1].shape[2:]
    width = min(4, n_blocks)
    ff = n_blocks * block
    return pl.pallas_call(
        functools.partial(low_kernel, pieces),
        grid_spec=pltpu.PrefetchScalarGridSpec(
            num_scalar_prefetch=1,
            grid=(n_blocks // width,),
            in_specs=[
                pl.BlockSpec((p.shape[0], 1, width, rows, block), lambda j, *_: (0, 0, j, 0, 0))
                for _, p in pieces
            ],
            out_specs=[
                pl.BlockSpec((width * block, rank), lambda j, *_: (j, 0)),
                pl.BlockSpec((rank, width * block), lambda j, *_: (0, j)),
            ],
            scratch_shapes=[pltpu.VMEM((width, shards, rows, block), BF16)],
        ),
        out_shape=[jax.ShapeDtypeStruct((ff, rank), F32), jax.ShapeDtypeStruct((rank, ff), F32)],
        compiler_params=params(),
        cost_estimate=COST,
    )(pos, *[p for _, p in pieces])


def gather_rows(value, shards):
    pos = lax.axis_index("dp")
    for bit in range(shards.bit_length() - 1)[::-1]:
        other = swap(value, "dp", 1 << bit)
        first = pos >> bit & 1 == 0
        pair = jnp.where(first, value, other), jnp.where(first, other, value)
        value = jnp.stack(pair, axis=shards.bit_length() - 1 - bit)
    return value


def per_device(hidden, cotangent, blocks, low_left, low_right):
    tok, ff = hidden.shape
    n_blocks, block = blocks.shape[1], blocks.shape[3]
    shards = lax.axis_size("dp")
    local_bits = n_blocks.bit_length() - 1
    cross_bits = lax.axis_size("tensor").bit_length() - 1
    n_local = 1 + local_bits
    scale = 1.0 / (tok * shards) ** 0.5
    pos = lax.axis_index("dp").astype(jnp.int32).reshape(1)

    factors = jnp.concatenate(
        [
            jnp.dot(hidden, low_left, preferred_element_type=F32),
            lax.dot_general(cotangent, low_right, NT, preferred_element_type=F32),
        ],
        axis=1,
    ).astype(BF16)
    rank = low_left.shape[1]

    def add(value, other):
        return (value.astype(F32) + other.astype(F32)).astype(BF16)

    cuts = [ff * quarter // 4 for quarter in range(5)]
    both = swap(jnp.stack([after(hidden, factors), cotangent]), "dp", 1)
    remote, ready = [], []
    for number, (start, stop) in enumerate(zip(cuts, cuts[1:])):
        part = after(hidden[:, start:stop], *ready, *([both] if ready else []))
        ready = [
            swap(
                jnp.concatenate([part, factors], axis=1) if bit == number < 2 else part,
                "tensor",
                1 << bit,
            )
            for bit in range(cross_bits)
        ]
        remote.append((stop - start, ready))
        if number < 2:
            factors = add(factors, ready[number][:, stop - start :])
        if number == 1:
            for bit in range(2, cross_bits):
                factors = add(factors, swap(factors, "tensor", 1 << bit))
    factor, back = factors[:, :rank], factors[:, rank:]

    pieces, gathered = gather_pieces(blocks, shards, remote[0][1] + remote[1][1])
    direct = gathered[1:3]
    distances = [0] + [1 << level for level in range(local_bits)]
    their_factors = swap(after(factors, *direct, *remote[1][1]), "dp", 1)
    kept = pair_grads(
        pos, (hidden, cotangent, factors), (both, both, their_factors), distances, n_blocks,
        shards, scale,
    )

    pieces = with_pair(pieces, [their_factors], remote[2][1] + [kept])
    cuts = [0, max(1, n_blocks * 7 // 16), max(2, n_blocks * 3 // 4), n_blocks]
    sent, returned, ready = [], [], remote[-1][1]
    for number, (start, stop) in enumerate(zip(cuts, cuts[1:])):
        terms = back_terms(
            pos, cotangent, pieces, n_local,
            cross_bits, shards, start, stop - start,
        )
        ready = [swap(after(t, *ready), "tensor", 1 << bit) for bit, t in enumerate(terms)]
        sent.append(list(terms))
        returned.append(ready)
    keep, send = block_grads(pos, after(cotangent, *sent[0]), remote, n_blocks, shards, scale)
    crossed = swap(send, "dp", 1)
    grads_local, received = scatter_sum(
        [kept], shards, gathered + remote[2][1] + sent[0], returned[0] + sent[1] + [keep]
    )
    mixed_rows, grad_in = rows_terms(
        pos, hidden, after(cotangent, *returned[0], crossed), factor, back, low_left, low_right, remote,
        pieces, distances, n_blocks, shards,
    )

    low = jnp.concatenate([part[n_local] for part in grads_local], axis=-1).astype(BF16)
    tie = received + returned[1] + sent[2] + [mixed_rows]
    if shards == 8:
        grads_cross, low_pieces = scatter_and_gather([keep, crossed], low, tie, returned[2])
        grad_left, grad_right = low_grads(pos, low_pieces, shards, rank)
    else:
        grads_cross, _ = scatter_sum([keep, crossed], shards, tie)
        low = gather_rows(low, shards).reshape(ff, 2 * rank).astype(F32)
        grad_left, grad_right = low[:, :rank], low[:, rank:].T
    grad_blocks = jnp.concatenate(
        [
            jnp.concatenate([a[:n_local], b], axis=0)
            for a, b in zip(grads_local, grads_cross)
        ],
        axis=-1,
    )

    returned = [jnp.concatenate(pair, axis=1) for pair in zip(*returned)]
    grad_hidden = (grad_in + sum(term.astype(F32) for term in returned)).astype(BF16)
    return (mixed_rows, grad_hidden, grad_blocks, grad_left, grad_right)


def solution(mesh):
    placed = (
        P("dp", "tensor"),
        P("dp", "tensor"),
        P(None, "tensor", "dp", None),
        P("tensor", None),
        P(None, "tensor"),
    )
    return jax.shard_map(
        per_device, mesh=mesh, in_specs=placed, out_specs=placed, check_vma=False
    )
```
